512 devices in a mesh: tm: 4 (over x), space: 128 (over z, y, core).
Axes of the slice: x: 4, y: 8, z: 8, core: 2. Of those that a mesh axis runs over, the one named last changes fastest.
Arguments:
- q_start: float32 [5, 512, 64, 128], P(None, 'space'), may hold values from -3.6 to 3.6
- guess: float32 [4, 5, 512, 64, 128], P('tm', None, 'space'), may hold values from -3.6 to 3.6
Outputs:
- corrected: float32 [4, 5, 512, 64, 128], P('tm', None, 'space')
- residual: float32 [4, 5, 512, 64, 128], P('tm', None, 'space')
The draws below stay inside these ranges and needn't reach their ends.
All inputs are finite; a program needn't handle non-finite values.
Results may differ from the reference program's by a relative error of at most 0.00011.
Values sent between devices are 32-bit elements; how exact they have to be, the bound alone decides.
No kernel may reach another device: no remote copies, remote signals or barrier semaphores. Data moves between devices by JAX's collectives and lax.ppermute only.
A program may use at most 64 MiB of HBM per device.

```python
import math
import jax
import jax.numpy as jnp
from jax import lax

BX = 4
NY = 64
NZ = 128
COMP = 5
STEPS_SLAB = 2
SWEEPS = 2
BLK = 4
NX = 512
SLABS = 4


def field_parts(key, slabs):
    keys = jax.random.split(key, 11)
    shape = (slabs, COMP, NX, NY, NZ)
    row_index = lax.broadcasted_iota(jnp.int32, shape, 2)
    col_index = lax.broadcasted_iota(jnp.int32, shape, 3)
    depth_index = lax.broadcasted_iota(jnp.int32, shape, 4)
    x_coord = (row_index.astype(jnp.float32) + 0.5) / NX
    y_coord = col_index.astype(jnp.float32) / NY
    z_coord = depth_index.astype(jnp.float32) / NZ
    modes = 3
    mode_shape = (modes, slabs, COMP, 1, 1, 1)
    wave_x = jax.random.randint(keys[0], mode_shape, 0, 3).astype(jnp.float32)
    wave_y = jax.random.randint(keys[1], mode_shape, 0, 3).astype(jnp.float32)
    wave_z = jax.random.randint(keys[2], mode_shape, 0, 3).astype(jnp.float32)
    phases = jax.random.uniform(keys[3], mode_shape, jnp.float32, 0.0, 2.0 * math.pi)
    weights = jax.random.uniform(keys[4], mode_shape, jnp.float32, 0.3, 0.5)
    smooth = jnp.zeros(shape, jnp.float32)
    for mode in range(modes):
        angle = math.pi * wave_x[mode] * x_coord + 2.0 * math.pi * (wave_y[mode] * y_coord + wave_z[mode] * z_coord) + phases[mode]
        smooth = smooth + weights[mode] * jnp.cos(angle)
    rough_flat = jax.random.uniform(keys[5], shape, jnp.float32, -0.9, 0.9)
    rough_normal = 0.5 * jax.random.truncated_normal(keys[6], -3.0, 3.0, shape, jnp.float32)
    level_signed = jax.random.uniform(keys[7], (slabs, COMP, 1, 1, 1), jnp.float32, -0.6, 0.6)
    level_plus = jax.random.uniform(keys[8], (slabs, COMP, 1, 1, 1), jnp.float32, 0.2, 1.4)
    block_shape = (slabs, COMP, NX // BX, 1, 1)
    block_offset = jax.random.uniform(keys[9], block_shape, jnp.float32, -0.8, 0.8)
    block_offset = jnp.repeat(block_offset, BX, axis=2)
    block_amplitude = jax.random.uniform(keys[10], block_shape, jnp.float32, 0.3, 1.6)
    block_amplitude = jnp.repeat(block_amplitude, BX, axis=2)
    return (smooth, rough_flat, rough_normal, level_signed, level_plus, block_offset, block_amplitude)


def compose(parts):
    smooth, rough_flat, rough_normal, level_signed, level_plus, block_offset, block_amplitude = parts
    value = level_signed + block_offset + smooth + block_amplitude * rough_normal
    return jnp.clip(value, -3.6, 3.6)


def draw_q_start(key, part):
    return compose(field_parts(jax.random.fold_in(key, 11), 1))[0]


def draw_guess(key, part):
    return compose(field_parts(jax.random.fold_in(key, 23), SLABS))


def setup_inputs(seed: int = 0) -> dict:
    seeds = jax.random.split(jax.random.key(seed), 3)
    return {
        "q_start": draw_q_start(jax.random.fold_in(seeds[2], 71), 0),
        "guess": draw_guess(jax.random.fold_in(seeds[2], 71), 0),
    }


time_step = 0.1
cross = 8.0
axial = 2.0
linear_rate = 0.1
quadratic_rate = 0.5
cubic_rate = 1.0


def bulk_terms(field):
    first, second, third, fourth, fifth = field[0], field[1], field[2], field[3], field[4]
    sixth = -first - fourth
    s_aa = first * first + second * second + third * third
    s_ab = first * second + second * fourth + third * fifth
    s_ac = first * third + second * fifth + third * sixth
    s_bb = second * second + fourth * fourth + fifth * fifth
    s_bc = second * third + fourth * fifth + fifth * sixth
    trace = first * first + fourth * fourth + sixth * sixth + 2.0 * (second * second + third * third + fifth * fifth)
    quad = jnp.stack([s_aa - trace / 3.0, s_ab, s_ac, s_bb - trace / 3.0, s_bc])
    source = field + time_step * quadratic_rate * quad
    diagonal = 1.0 + time_step * (linear_rate + cubic_rate * trace) + 2.0 * (2.0 * cross + axial)
    return source, diagonal


def jacobi_sweep(current, source, diagonal):
    padded = jnp.pad(current, ((0, 0), (1, 1), (1, 1), (0, 0)))
    along_x = padded[:, :-2, 1:-1] + padded[:, 2:, 1:-1]
    along_y = padded[:, 1:-1, :-2] + padded[:, 1:-1, 2:]
    along_z = jnp.roll(current, 1, 3) + jnp.roll(current, -1, 3)
    return (source + cross * (along_x + along_y) + axial * along_z) / diagonal[None]


def implicit_step(field):
    source, diagonal = bulk_terms(field)
    current = field
    for sweep in range(SWEEPS):
        current = jacobi_sweep(current, source, diagonal)
    return current


def propagate(field):
    for step in range(STEPS_SLAB):
        field = implicit_step(field)
    return field


def restrict(field):
    total = jnp.sum(field, axis=(1, 2))
    total = total.reshape(COMP, NZ // BLK, BLK).sum(axis=2)
    return total / (NX * NY * BLK)


def reference(q_start, guess):
    starts = jnp.concatenate([q_start[None], guess[:-1]], axis=0)
    relaxed = lax.map(propagate, starts)
    starts_two = jnp.concatenate([q_start[None], relaxed[:-1]], axis=0)
    again = lax.map(propagate, starts_two)
    residual = again - relaxed
    change = again - guess
    coarse = lax.map(restrict, change)
    decay = 1.0 / (1.0 + STEPS_SLAB * time_step * linear_rate)

    def advance(error, term):
        error = decay * error + term
        return error, error

    zero_error = jnp.zeros((COMP, NZ // BLK), jnp.float32)
    last, errors = lax.scan(advance, zero_error, coarse)
    spread = jnp.broadcast_to(errors[:, :, None, None, :, None], (SLABS, COMP, 1, 1, NZ // BLK, BLK))
    spread = spread.reshape(SLABS, COMP, 1, 1, NZ)
    corrected = relaxed + spread
    return corrected, residual
```

```python
import jax
import jax.numpy as jnp
import numpy as np
from jax import lax
from jax.experimental import pallas as pl
from jax.experimental.pallas import tpu as pltpu
from jax.sharding import Mesh
from jax.sharding import PartitionSpec as P

COMP = 5
STEPS_SLAB = 2
BLK = 4
ROWS = 4
PAD = 8
GROUP = 16

time_step = 0.1
cross = 8.0
axial = 2.0
linear_rate = 0.1
quadratic_rate = 0.5
cubic_rate = 1.0

SPACE = ("outer", "inner")


def phi_rows(first, last, w, v, src, rdg, emit, ny):
    ys = pl.ds(PAD, ny)
    low_mask = jnp.where(first, 0.0, 1.0)
    high_mask = jnp.where(last, 0.0, 1.0)

    def bulk(row):
        part = 32
        for y in range(0, ny, part):
            at = pl.ds(PAD + y, part)
            q = [w[c, row, at, :] for c in range(COMP)]
            a, b, c, d, e = q
            f = -a - d
            aa, bb, cc, dd, ee = a * a, b * b, c * c, d * d, e * e
            trace = aa + dd + f * f + 2.0 * (bb + cc + ee)
            third = trace * (1.0 / 3.0)
            quad = (
                aa + bb + cc - third,
                a * b + b * d + c * e,
                a * c + b * e + c * f,
                bb + dd + ee - third,
                b * c + d * e + e * f,
            )
            out = pl.ds(y, part)
            for k in range(COMP):
                src[k, row, out, :] = (1.0 / cross) * q[k] + (time_step * quadratic_rate / cross) * quad[k]
            scale = cross
            if row < ROWS:
                scale = cross * low_mask
            if row >= 2 * ROWS:
                scale = cross * high_mask
            diagonal = (1.0 + time_step * linear_rate + 2.0 * (2.0 * cross + axial)) + (time_step * cubic_rate) * trace
            rdg[row, out, :] = scale / diagonal

    def sweep(a, rows, store):
        for row in rows:
            rd = rdg[row]
            for k in range(COMP):
                here = a[k, row, ys, :]
                along_x = a[k, row - 1, ys, :] + a[k, row + 1, ys, :]
                along_y = a[k, row, pl.ds(PAD - 1, ny), :] + a[k, row, pl.ds(PAD + 1, ny), :]
                along_z = pltpu.roll(here, 1, 1) + pltpu.roll(here, here.shape[1] - 1, 1)
                store(k, row, (src[k, row] + (along_x + along_y) + (axial / cross) * along_z) * rd)

    def into(buf):
        def store(k, row, value):
            buf[k, row, ys, :] = value

        return store

    for row in range(1, 3 * ROWS - 1):
        bulk(row)
    sweep(w, range(1, 11), into(v))
    sweep(v, range(2, 10), into(w))
    for row in range(3, 9):
        bulk(row)
    sweep(w, range(3, 9), into(v))
    sweep(v, range(4, 8), emit)


def place():
    outer, inner = lax.axis_index("outer"), lax.axis_index("inner")
    count = lax.axis_size("outer") * lax.axis_size("inner")
    index = outer * lax.axis_size("inner") + inner
    return index, count


def gather_rows(own, near, far, w, v, sems, ny):
    index, count = place()
    odd = index % 2
    near_at = jnp.where(odd == 1, 0, 2 * ROWS)
    far_at = jnp.where(odd == 1, 2 * ROWS, 0)
    ys = pl.ds(PAD, ny)
    copies = [
        pltpu.make_async_copy(own, w.at[:, pl.ds(ROWS, ROWS), ys, :], sems.at[0]),
        pltpu.make_async_copy(near, w.at[:, pl.ds(near_at, ROWS), ys, :], sems.at[1]),
        pltpu.make_async_copy(far, w.at[:, pl.ds(far_at, ROWS), ys, :], sems.at[2]),
    ]
    for copy in copies:
        copy.start()
    zero = jnp.zeros((COMP, 3 * ROWS, PAD, w.shape[3]), jnp.float32)
    for buf in (w, v):
        buf[:, :, pl.ds(0, PAD), :] = zero
        buf[:, :, pl.ds(PAD + ny, PAD), :] = zero
    for copy in copies:
        copy.wait()
    return index == 0, index == count - 1


def first_kernel(own, near, far, out, w, v, src, rdg, sems):
    ny = out.shape[2]
    first, last = gather_rows(own, near, far, w, v, sems, ny)

    def emit(k, row, value):
        out[k, row - ROWS] = value

    phi_rows(first, last, w, v, src, rdg, emit, ny)


def exact_dot(a, b):
    return jnp.dot(a, b, precision=lax.Precision.HIGHEST, preferred_element_type=jnp.float32)


def second_kernel(own, near, far, guess, weights, out, share, w, v, src, rdg, sems):
    ny, nz = out.shape[2], out.shape[3]
    first, last = gather_rows(own, near, far, w, v, sems, ny)
    sums = []
    for k in range(COMP):
        mine = [w[k, ROWS + r, pl.ds(PAD, ny), :] for r in range(ROWS)]
        sums.append(
            (
                jnp.sum(sum(mine[1:], mine[0]), axis=0, keepdims=True),
                jnp.sum(jnp.sum(guess[0, k], axis=0), axis=0, keepdims=True),
            )
        )
    total = [jnp.zeros((ny, nz), jnp.float32) for _ in range(COMP)]

    def emit(k, row, value):
        out[k, row - ROWS] = value
        total[k] = total[k] + value

    phi_rows(first, last, w, v, src, rdg, emit, ny)
    none = jnp.zeros((8 - COMP, nz), jnp.float32)

    def rows(parts):
        return jnp.concatenate(parts + [none], axis=0)

    slab = lax.axis_index("tm")
    blocks = nz // BLK
    cell = lax.broadcasted_iota(jnp.int32, (nz, nz), 0) // BLK
    slot = lax.broadcasted_iota(jnp.int32, (nz, nz), 1) % blocks
    pick = jnp.where(cell == slot, 1.0, 0.0)
    again = exact_dot(rows([jnp.sum(t, axis=0, keepdims=True) for t in total]), pick)
    relaxed = exact_dot(rows([s[0] for s in sums]), pick)
    old = exact_dot(rows([s[1] for s in sums]), pick)
    weight = weights[slab]
    value = weight[0:1] * again + weight[1:2] * relaxed + weight[2:3] * old
    for i in range(share.shape[0]):
        share[i] = value


def relay_kernel(parts, share):
    value = parts[0]
    for i in range(1, parts.shape[0]):
        value = value + parts[i]
    for i in range(share.shape[0]):
        share[i] = value


def last_kernel(parts, relaxed, again, corrected, residual, error):
    nz = relaxed.shape[3]
    slab = lax.axis_index("tm")
    k = pl.program_id(0)

    @pl.when(k == 0)
    def _():
        value = parts[0]
        for i in range(1, parts.shape[0]):
            value = value + parts[i]
        blocks = nz // BLK
        slot = lax.broadcasted_iota(jnp.int32, (nz, nz), 0)
        cell = lax.broadcasted_iota(jnp.int32, (nz, nz), 1) // BLK
        error[...] = exact_dot(value, jnp.where(slot == slab * blocks + cell, 1.0, 0.0))

    mine = relaxed[0]
    other = jnp.where(slab == 0, mine, again[0])
    corrected[0, 0] = mine + error[pl.ds(k, 1), :][None]
    residual[0, 0] = other - mine


def slot_weights(slabs, nz, cells):
    decay = 1.0 / (1.0 + STEPS_SLAB * time_step * linear_rate)
    table = np.zeros((slabs, 8, nz))
    blocks = nz // BLK
    for own in range(slabs):
        chain = (own + 1) % slabs
        slots = {2: (own, -1.0)}
        if chain + 1 < slabs:
            slots[0] = (chain + 1, 1.0)
        if chain == 0:
            slots[1] = (0, 1.0)
        for which, (slot, sign) in slots.items():
            for target in range(slot, slabs):
                table[own, which, target * blocks : (target + 1) * blocks] = sign * decay ** (target - slot) / cells
    return jnp.asarray(table, jnp.float32)


def swapped(block, count):
    near = [(i, i ^ 1) for i in range(count)]
    far = []
    for i in range(1, count - 1, 2):
        far += [(i, i + 1), (i + 1, i)]
    from_far = lax.ppermute(block, SPACE, far)
    from_near = lax.ppermute(block, SPACE, near)
    return from_near, from_far


def per_device(q_start, guess):
    own = guess[0]
    slabs = lax.axis_size("tm")
    count = lax.axis_size("outer") * lax.axis_size("inner")
    _, rows, ny, nz = own.shape
    field = jax.ShapeDtypeStruct(own.shape, jnp.float32)
    any_spec = pl.BlockSpec(memory_space=pl.ANY)
    scratch = [
        pltpu.VMEM((COMP, 3 * ROWS, ny + 2 * PAD, nz), jnp.float32),
        pltpu.VMEM((COMP, 3 * ROWS, ny + 2 * PAD, nz), jnp.float32),
        pltpu.VMEM((COMP, 3 * ROWS, ny, nz), jnp.float32),
        pltpu.VMEM((3 * ROWS, ny, nz), jnp.float32),
        pltpu.SemaphoreType.DMA((3,)),
    ]
    tile = (8, nz)

    start = jnp.where(lax.axis_index("tm") == slabs - 1, q_start, own)
    near, far = swapped(start, count)
    relaxed = pl.pallas_call(
        first_kernel, out_shape=field, in_specs=[any_spec] * 3, scratch_shapes=scratch, name="relax"
    )(start, near, far)

    near, far = swapped(relaxed, count)
    my_relaxed = lax.ppermute(relaxed, "tm", [(i, (i + 1) % slabs) for i in range(slabs)])
    weights = slot_weights(slabs, nz, count * rows * ny * BLK)
    vmem = pl.BlockSpec(memory_space=pltpu.VMEM)
    again, share = pl.pallas_call(
        second_kernel,
        out_shape=(field, jax.ShapeDtypeStruct((GROUP, *tile), jnp.float32)),
        in_specs=[any_spec] * 3 + [vmem, vmem],
        scratch_shapes=scratch,
        name="again",
    )(relaxed, near, far, guess, weights)

    my_again = lax.ppermute(again, "tm", [(i, (i + 2) % slabs) for i in range(slabs)])
    parts = lax.all_to_all(share, "inner", 0, 0)
    wide = slabs * lax.axis_size("outer")
    share = pl.pallas_call(
        relay_kernel, out_shape=jax.ShapeDtypeStruct((wide, *tile), jnp.float32), name="relay"
    )(parts)
    parts = lax.all_to_all(share, ("tm", "outer"), 0, 0)

    block = pl.BlockSpec((1, rows, ny, nz), lambda k: (k, 0, 0, 0))
    block_out = pl.BlockSpec((1, 1, rows, ny, nz), lambda k: (0, k, 0, 0, 0))
    out = jax.ShapeDtypeStruct((1, *own.shape), jnp.float32)
    corrected, residual = pl.pallas_call(
        last_kernel,
        out_shape=(out, out),
        grid=(COMP,),
        in_specs=[pl.BlockSpec((wide, *tile), lambda k: (0, 0, 0)), block, block],
        out_specs=(block_out, block_out),
        scratch_shapes=[pltpu.VMEM(tile, jnp.float32)],
        name="correct",
    )(parts, my_relaxed, my_again)
    return corrected, residual


def solution(mesh):
    slabs, count = mesh.shape["tm"], mesh.shape["space"]
    fine = Mesh(mesh.devices.reshape(slabs, count // GROUP, GROUP), ("tm", *SPACE))
    q_spec = P(None, SPACE, None, None)
    field_spec = P("tm", None, SPACE, None, None)
    return jax.shard_map(
        per_device,
        mesh=fine,
        in_specs=(q_spec, field_spec),
        out_specs=(field_spec, field_spec),
        check_vma=False,
    )
```

```python
import jax
import jax.numpy as jnp
import numpy as np
from jax import lax
from jax.experimental import pallas as pl
from jax.experimental.pallas import tpu as pltpu
from jax.sharding import Mesh
from jax.sharding import PartitionSpec as P

COMP = 5
STEPS_SLAB = 2
BLK = 4
ROWS = 4
SUB = 8
GROUP = 16

time_step = 0.1
cross = 8.0
axial = 2.0
linear_rate = 0.1
quadratic_rate = 0.5
cubic_rate = 1.0

SPACE = ("outer", "inner")
LIMIT = pltpu.CompilerParams(vmem_limit_bytes=16 * 1024 * 1024)


def index_in_space():
    return lax.axis_index("outer") * lax.axis_size("inner") + lax.axis_index("inner")


def row_of():
    odd = index_in_space() % 2 == 1
    return lambda i: jnp.where(odd, ROWS - 1 - i, i)


def spaced(ref, k, row):
    count = ref.shape[2] // SUB
    return jnp.stack([ref[k, row, pl.ds(v, SUB, stride=count), :] for v in range(count)])


def bulk(q, scale):
    a, b, c, d, e = q
    f = a + d
    aa, bb, cc, dd, ee = a * a, b * b, c * c, d * d, e * e
    off = bb + cc
    trace = aa + dd + f * f + 2.0 * (off + ee)
    third = trace * (1.0 / 3.0)
    quad = (aa + off - third, b * f + c * e, b * e - c * d, bb + dd + ee - third, b * c - a * e)
    source = [(1.0 / cross) * q[k] + (time_step * quadratic_rate / cross) * quad[k] for k in range(COMP)]
    constant = 1.0 + time_step * linear_rate + 2.0 * (2.0 * cross + axial)
    return source, scale / (constant + (time_step * cubic_rate) * trace)


def bulk_row(read, write_source, write_scale, count, scale):
    part = 2
    for v in range(0, count, part):
        at = pl.ds(v, part)
        source, ratio = bulk([read(k, at) for k in range(COMP)], scale)
        for k in range(COMP):
            write_source(k, at, source[k])
        write_scale(at, ratio)


def relaxed_row(here, low, high, source, scale):
    count, sub, nz = here.shape
    lane_of = lax.broadcasted_iota(jnp.int32, (sub, nz), 0)
    before = jnp.where(lane_of == 0, 0.0, pltpu.roll(here[count - 1], 1, 0))
    after = jnp.where(lane_of == sub - 1, 0.0, pltpu.roll(here[0], sub - 1, 0))
    along_y = jnp.concatenate([before[None], here[:-1]], axis=0) + jnp.concatenate([here[1:], after[None]], axis=0)
    along_z = pltpu.roll(here, 1, 2) + pltpu.roll(here, nz - 1, 2)
    return (source + ((low + high) + along_y) + (axial / cross) * along_z) * scale


def prepare_rows(own, packed, source, scale):
    row = row_of()
    for i in range(ROWS):
        r = row(i)
        for k in range(COMP):
            packed[k, r] = spaced(own, k, r)

        def write_source(k, at, value, i=i):
            source[k, i, at] = value

        def write_scale(at, value, i=i):
            scale[i, at] = value

        bulk_row(lambda k, at, r=r: packed[k, r, at], write_source, write_scale, packed.shape[2], cross)


def prepare_kernel(own, packed, source, scale):
    prepare_rows(own, packed, source, scale)


def packed_sums(rows):
    nz = rows[0].shape[1]
    value = jnp.concatenate(rows + [jnp.zeros((SUB - COMP, nz), jnp.float32)], axis=0)
    total = value
    for i in range(1, BLK):
        total = total + pltpu.roll(value, nz - i, 1)
    blocks = nz // BLK
    lane = lax.broadcasted_iota(jnp.int32, (SUB, nz), 1)
    sub = lax.broadcasted_iota(jnp.int32, (SUB, nz), 0)
    total = jnp.take_along_axis(total, BLK * (lane % blocks), axis=1)
    first = jnp.sum(jnp.where(lane // blocks == sub, total, 0.0)[:BLK], axis=0, keepdims=True)
    second = jnp.where(lane[:1] < blocks, total[COMP - 1 : COMP], 0.0)
    return jnp.where(sub % 2 == 0, first, second)


def field_sums(field):
    return [jnp.sum(jnp.sum(field(k), axis=0), axis=0, keepdims=True) for k in range(COMP)]


def prepare_again_kernel(own, guess, weights, packed, source, scale, rest):
    prepare_rows(own, packed, source, scale)
    slab = lax.axis_index("tm")
    relaxed = packed_sums(field_sums(lambda k: own[k]))
    old = packed_sums(field_sums(lambda k: guess[0, k]))
    rest[...] = weights[slab, 1] * relaxed + weights[slab, 2] * old


def near_kernel(packed, near, source, scale, v1, w2, source2, scale2, v2, near_source, near_scale, v1_more, w2_more):
    row = row_of()
    count = packed.shape[2]
    for i in range(3):

        def write_source(k, at, value, i=i):
            near_source[k, i, at] = value

        def write_scale(at, value, i=i):
            near_scale[i, at] = value

        r = row(i)
        bulk_row(lambda k, at, r=r: near[k, r, at], write_source, write_scale, count, cross)

    def w_at(k, r):
        return packed[k, row(r - 4)] if r < 8 else near[k, row(r - 8)]

    def source_at(k, r):
        return source[k, r - 4] if r < 8 else near_source[k, r - 8]

    def scale_at(r):
        return scale[r - 4] if r < 8 else near_scale[r - 8]

    for r in range(5, 11):
        for k in range(COMP):
            value = relaxed_row(w_at(k, r), w_at(k, r - 1), w_at(k, r + 1), source_at(k, r), scale_at(r))
            if r < 7:
                v1[k, r - 5] = value
            else:
                v1_more[k, r - 7] = value

    def v1_at(k, r):
        return v1[k, r - 5] if r < 7 else v1_more[k, r - 7]

    for r in range(6, 10):
        for k in range(COMP):
            value = relaxed_row(v1_at(k, r), v1_at(k, r - 1), v1_at(k, r + 1), source_at(k, r), scale_at(r))
            if r < 8:
                w2[k, r - 6] = value
            else:
                w2_more[k, r - 8] = value

    def w2_at(k, r):
        return w2[k, r - 6] if r < 8 else w2_more[k, r - 8]

    for r in range(6, 9):

        def read(k, at, r=r):
            return w2[k, r - 6, at] if r < 8 else w2_more[k, r - 8, at]

        def write_source(k, at, value, r=r):
            if r < 8:
                source2[k, r - 6, at] = value
            else:
                near_source[k, 0, at] = value

        def write_scale(at, value, r=r):
            if r < 8:
                scale2[r - 6, at] = value
            else:
                near_scale[0, at] = value

        bulk_row(read, write_source, write_scale, count, cross)
    for r in range(7, 9):
        for k in range(COMP):
            src = source2[k, r - 6] if r < 8 else near_source[k, 0]
            scl = scale2[r - 6] if r < 8 else near_scale[0]
            v2[k, r - 7] = relaxed_row(w2_at(k, r), w2_at(k, r - 1), w2_at(k, r + 1), src, scl)


def far_rows(packed, far, source, scale, v1, w2, source2, scale2, v2, work, emit):
    wf, far_source, far_scale, v1_far, w2_far, source2_far, scale2_far, v2_far = work
    row = row_of()
    count = packed.shape[2]
    index = index_in_space()
    edge = (index == 0) | (index == lax.axis_size("outer") * lax.axis_size("inner") - 1)
    masked = jnp.where(edge, 0.0, cross)
    for j in range(ROWS):
        for k in range(COMP):
            wf[k, j] = spaced(far, k, row(j))
    for r in range(1, 4):

        def write_source(k, at, value, r=r):
            far_source[k, r - 1, at] = value

        def write_scale(at, value, r=r):
            far_scale[r - 1, at] = value

        bulk_row(lambda k, at, r=r: wf[k, r, at], write_source, write_scale, count, masked)

    def w_at(k, r):
        return wf[k, r] if r < 4 else packed[k, row(r - 4)]

    def source_at(k, r):
        return far_source[k, r - 1] if r < 4 else source[k, r - 4]

    def scale_at(r):
        return far_scale[r - 1] if r < 4 else scale[r - 4]

    for r in range(1, 5):
        for k in range(COMP):
            v1_far[k, r - 1] = relaxed_row(w_at(k, r), w_at(k, r - 1), w_at(k, r + 1), source_at(k, r), scale_at(r))

    def v1_at(k, r):
        return v1_far[k, r - 1] if r < 5 else v1[k, r - 5]

    for r in range(2, 6):
        for k in range(COMP):
            w2_far[k, r - 2] = relaxed_row(v1_at(k, r), v1_at(k, r - 1), v1_at(k, r + 1), source_at(k, r), scale_at(r))
    for r in range(3, 6):

        def write_source(k, at, value, r=r):
            source2_far[k, r - 3, at] = value

        def write_scale(at, value, r=r):
            scale2_far[r - 3, at] = value

        bulk_row(
            lambda k, at, r=r: w2_far[k, r - 2, at], write_source, write_scale, count, masked if r < 4 else cross
        )

    def w2_at(k, r):
        return w2_far[k, r - 2] if r < 6 else w2[k, r - 6]

    def source2_at(k, r):
        return source2_far[k, r - 3] if r < 6 else source2[k, r - 6]

    def scale2_at(r):
        return scale2_far[r - 3] if r < 6 else scale2[r - 6]

    for r in range(3, 7):
        for k in range(COMP):
            v2_far[k, r - 3] = relaxed_row(
                w2_at(k, r), w2_at(k, r - 1), w2_at(k, r + 1), source2_at(k, r), scale2_at(r)
            )

    def v2_at(k, r):
        return v2_far[k, r - 3] if r < 7 else v2[k, r - 7]

    for r in range(4, 8):
        for k in range(COMP):
            value = relaxed_row(v2_at(k, r), v2_at(k, r - 1), v2_at(k, r + 1), source2_at(k, r), scale2_at(r))
            emit(k, row(r - 4), value)


def store_spaced(out, k, row, value):
    count = value.shape[0]
    for v in range(count):
        out[k, row, pl.ds(v, SUB, stride=count), :] = value[v]


def far_kernel(packed, far, source, scale, v1, w2, source2, scale2, v2, out, *work):
    def emit(k, row, value):
        store_spaced(out, k, row, value)

    far_rows(packed, far, source, scale, v1, w2, source2, scale2, v2, work, emit)


def far_again_kernel(packed, far, source, scale, v1, w2, source2, scale2, v2, rest, weights, out, share, *work):
    nz = out.shape[3]
    total = [jnp.zeros((SUB, nz), jnp.float32) for _ in range(COMP)]

    def emit(k, row, value):
        store_spaced(out, k, row, value)
        total[k] = total[k] + jnp.sum(value, axis=0)

    far_rows(packed, far, source, scale, v1, w2, source2, scale2, v2, work, emit)
    again = packed_sums([jnp.sum(t, axis=0, keepdims=True) for t in total])
    value = weights[lax.axis_index("tm"), 0] * again + rest[...]
    for i in range(share.shape[0]):
        share[i] = value


def relay_kernel(parts, share):
    value = parts[0]
    for i in range(1, parts.shape[0]):
        value = value + parts[i]
    sub = lax.broadcasted_iota(jnp.int32, value.shape, 0)
    slabs = SUB // 2
    each = share.shape[0] // slabs
    for p in range(slabs):
        pair = jnp.where(sub % 2 == 0, value[2 * p : 2 * p + 1], value[2 * p + 1 : 2 * p + 2])
        for i in range(0, each, SUB):
            share[pl.ds(p * each + i, SUB), :] = pair


def residual_kernel(relaxed, again, residual):
    slab = lax.axis_index("tm")
    for k in range(COMP):
        mine = relaxed[k]
        residual[0, k] = jnp.where(slab == 0, mine, again[k]) - mine


def correct_kernel(parts, relaxed, corrected):
    value = parts[pl.ds(0, SUB), :]
    for i in range(SUB, parts.shape[0], SUB):
        value = value + parts[pl.ds(i, SUB), :]
    value = value + pltpu.roll(value, 4, 0)
    value = value + pltpu.roll(value, 2, 0)
    nz = value.shape[1]
    lane = lax.broadcasted_iota(jnp.int32, value.shape, 1)
    for k in range(COMP):
        spread = jnp.take_along_axis(value, (k % BLK) * (nz // BLK) + lane // BLK, axis=1)
        which = k // BLK
        corrected[0, k] = relaxed[k] + spread[which : which + 1][None]


def slot_weights(slabs, nz, cells):
    decay = 1.0 / (1.0 + STEPS_SLAB * time_step * linear_rate)
    table = np.zeros((slabs, 3, SUB, nz))
    for own in range(slabs):
        chain = (own + 1) % slabs
        slots = {2: (own, -1.0)}
        if chain + 1 < slabs:
            slots[0] = (chain + 1, 1.0)
        if chain == 0:
            slots[1] = (0, 1.0)
        for which, (slot, sign) in slots.items():
            for target in range(slot, slabs):
                table[own, which, 2 * target : 2 * target + 2] = sign * decay ** (target - slot) / cells
    return jnp.asarray(table, jnp.float32)


def f32(*shape):
    return jax.ShapeDtypeStruct(shape, jnp.float32)


def call(kernel, name, out, inputs, scratch=()):
    vmem = pl.BlockSpec(memory_space=pltpu.VMEM)
    return pl.pallas_call(
        kernel,
        out_shape=out,
        in_specs=[vmem] * len(inputs),
        out_specs=jax.tree.map(lambda _: vmem, out),
        scratch_shapes=list(scratch),
        compiler_params=LIMIT,
        name=name,
    )(*inputs)


def per_device(q_start, guess):
    own = guess[0]
    slabs = lax.axis_size("tm")
    count = lax.axis_size("outer") * lax.axis_size("inner")
    _, rows, ny, nz = own.shape
    row = (ny // SUB, SUB, nz)
    near_pairs = [(i, i ^ 1) for i in range(count)]
    far_pairs = []
    for i in range(1, count - 1, 2):
        far_pairs += [(i, i + 1), (i + 1, i)]

    def several(*lead):
        return f32(*lead, *row)

    def scratch(*lead):
        return pltpu.VMEM((*lead, *row), jnp.float32)

    prepared = (several(COMP, ROWS), several(COMP, ROWS), several(ROWS))
    state = (several(COMP, 2), several(COMP, 2), several(COMP, 2), several(2), several(COMP, 2))
    near_scratch = (scratch(COMP, 3), scratch(3), scratch(COMP, 4), scratch(COMP, 2))
    far_scratch = (
        scratch(COMP, ROWS),
        scratch(COMP, 3),
        scratch(3),
        scratch(COMP, 4),
        scratch(COMP, 4),
        scratch(COMP, 3),
        scratch(3),
        scratch(COMP, 4),
    )

    start = jnp.where(lax.axis_index("tm") == slabs - 1, q_start, own)
    far = lax.ppermute(start, SPACE, far_pairs)
    packed, source, scale = call(prepare_kernel, "prepare", prepared, (start,))
    near = lax.ppermute(packed, SPACE, near_pairs)
    kept = call(near_kernel, "near", state, (packed, near, source, scale), near_scratch)
    relaxed = call(far_kernel, "far", f32(*own.shape), (packed, far, source, scale, *kept), far_scratch)

    far = lax.ppermute(relaxed, SPACE, far_pairs)
    my_relaxed = lax.ppermute(relaxed, "tm", [(i, (i + 1) % slabs) for i in range(slabs)])
    weights = slot_weights(slabs, nz, count * rows * ny * BLK)
    packed, source, scale, rest = call(
        prepare_again_kernel, "prepare_again", (*prepared, f32(SUB, nz)), (relaxed, guess, weights)
    )
    near = lax.ppermute(packed, SPACE, near_pairs)
    kept = call(near_kernel, "near", state, (packed, near, source, scale), near_scratch)
    again, share = call(
        far_again_kernel,
        "far_again",
        (f32(*own.shape), f32(GROUP, SUB, nz)),
        (packed, far, source, scale, *kept, rest, weights),
        far_scratch,
    )

    my_again = lax.ppermute(again, "tm", [(i, (i + 2) % slabs) for i in range(slabs)])
    parts = lax.all_to_all(share, "inner", 0, 0)
    wide = slabs * lax.axis_size("outer")
    share = call(relay_kernel, "relay", f32(2 * wide, nz), (parts,))
    parts = lax.all_to_all(share.reshape(wide, 2, nz), ("tm", "outer"), 0, 0).reshape(2 * wide, nz)
    residual = call(residual_kernel, "residual", f32(1, *own.shape), (my_relaxed, my_again))
    corrected = call(correct_kernel, "correct", f32(1, *own.shape), (parts, my_relaxed))
    return corrected, residual


def solution(mesh):
    slabs, count = mesh.shape["tm"], mesh.shape["space"]
    fine = Mesh(mesh.devices.reshape(slabs, count // GROUP, GROUP), ("tm", *SPACE))
    q_spec = P(None, SPACE, None, None)
    field_spec = P("tm", None, SPACE, None, None)
    return jax.shard_map(
        per_device,
        mesh=fine,
        in_specs=(q_spec, field_spec),
        out_specs=(field_spec, field_spec),
        check_vma=False,
    )
```

```python
import jax
import jax.numpy as jnp
import numpy as np
from jax import lax
from jax.experimental import pallas as pl
from jax.experimental.pallas import tpu as pltpu
from jax.sharding import Mesh
from jax.sharding import PartitionSpec as P

COMP = 5
STEPS_SLAB = 2
BLK = 4
ROWS = 4
SUB = 8
GROUP = 16

time_step = 0.1
cross = 8.0
axial = 2.0
linear_rate = 0.1
quadratic_rate = 0.5
cubic_rate = 1.0

SPACE = ("outer", "inner")
LIMIT = pltpu.CompilerParams(vmem_limit_bytes=16 * 1024 * 1024)


def index_in_space():
    return lax.axis_index("outer") * lax.axis_size("inner") + lax.axis_index("inner")


def row_of():
    odd = index_in_space() % 2 == 1
    return lambda i: jnp.where(odd, ROWS - 1 - i, i)


def spaced(ref, k, row):
    count = ref.shape[2] // SUB
    return jnp.stack([ref[k, row, pl.ds(v, SUB, stride=count), :] for v in range(count)])


def bulk(q, scale):
    a, b, c, d, e = q
    f = a + d
    aa, bb, cc, dd, ee = a * a, b * b, c * c, d * d, e * e
    off = bb + cc
    trace = aa + dd + f * f + 2.0 * (off + ee)
    third = trace * (1.0 / 3.0)
    quad = (aa + off - third, b * f + c * e, b * e - c * d, bb + dd + ee - third, b * c - a * e)
    source = [(1.0 / cross) * q[k] + (time_step * quadratic_rate / cross) * quad[k] for k in range(COMP)]
    constant = 1.0 + time_step * linear_rate + 2.0 * (2.0 * cross + axial)
    return source, scale / (constant + (time_step * cubic_rate) * trace)


def bulk_row(read, write_source, write_scale, count, scale):
    part = 2
    for v in range(0, count, part):
        at = pl.ds(v, part)
        source, ratio = bulk([read(k, at) for k in range(COMP)], scale)
        for k in range(COMP):
            write_source(k, at, source[k])
        write_scale(at, ratio)


def relaxed_row(here, low, high, source, scale):
    count, sub, nz = here.shape
    lane_of = lax.broadcasted_iota(jnp.int32, (sub, nz), 0)
    before = jnp.where(lane_of == 0, 0.0, pltpu.roll(here[count - 1], 1, 0))
    after = jnp.where(lane_of == sub - 1, 0.0, pltpu.roll(here[0], sub - 1, 0))
    along_y = jnp.concatenate([before[None], here[:-1]], axis=0) + jnp.concatenate([here[1:], after[None]], axis=0)
    along_z = pltpu.roll(here, 1, 2) + pltpu.roll(here, nz - 1, 2)
    return (source + ((low + high) + along_y) + (axial / cross) * along_z) * scale


def prepare_rows(own, packed, source, scale):
    row = row_of()
    for i in range(ROWS):
        half, j = packed[i // 2], i % 2
        for k in range(COMP):
            half[k, j] = spaced(own, k, row(i))

        def write_source(k, at, value, i=i):
            source[k, i, at] = value

        def write_scale(at, value, i=i):
            scale[i, at] = value

        def read(k, at, half=half, j=j):
            return half[k, j, at]

        bulk_row(read, write_source, write_scale, half.shape[2], cross)


def prepare_kernel(own, outer, inner, source, scale):
    prepare_rows(own, (outer, inner), source, scale)


def packed_sums(rows):
    nz = rows[0].shape[1]
    value = jnp.concatenate(rows + [jnp.zeros((SUB - COMP, nz), jnp.float32)], axis=0)
    total = value
    for i in range(1, BLK):
        total = total + pltpu.roll(value, nz - i, 1)
    blocks = nz // BLK
    lane = lax.broadcasted_iota(jnp.int32, (SUB, nz), 1)
    sub = lax.broadcasted_iota(jnp.int32, (SUB, nz), 0)
    total = jnp.take_along_axis(total, BLK * (lane % blocks), axis=1)
    first = jnp.sum(jnp.where(lane // blocks == sub, total, 0.0)[:BLK], axis=0, keepdims=True)
    second = jnp.where(lane[:1] < blocks, total[COMP - 1 : COMP], 0.0)
    return jnp.where(sub % 2 == 0, first, second)


def field_sums(field):
    return [jnp.sum(jnp.sum(field(k), axis=0), axis=0, keepdims=True) for k in range(COMP)]


def prepare_again_kernel(own, guess, weights, outer, inner, source, scale, rest):
    prepare_rows(own, (outer, inner), source, scale)
    slab = lax.axis_index("tm")
    relaxed = packed_sums(field_sums(lambda k: own[k]))
    old = packed_sums(field_sums(lambda k: guess[0, k]))
    rest[...] = weights[slab, 1] * relaxed + weights[slab, 2] * old


def near_kernel(outer, inner, near_outer, near_inner, source, scale, v1, w2, source2, scale2, v2, near_source, near_scale, v1_more, w2_more):
    count = outer.shape[2]

    def w_at(k, r, at=slice(None)):
        if r < 8:
            return (outer if r < 6 else inner)[k, r % 2, at]
        r = 11 - r
        return (near_outer if r < 2 else near_inner)[k, r % 2, at]

    for i in range(3):

        def write_source(k, at, value, i=i):
            near_source[k, i, at] = value

        def write_scale(at, value, i=i):
            near_scale[i, at] = value

        bulk_row(lambda k, at, i=i: w_at(k, 8 + i, at), write_source, write_scale, count, cross)

    def source_at(k, r):
        return source[k, r - 4] if r < 8 else near_source[k, r - 8]

    def scale_at(r):
        return scale[r - 4] if r < 8 else near_scale[r - 8]

    for r in range(5, 11):
        for k in range(COMP):
            value = relaxed_row(w_at(k, r), w_at(k, r - 1), w_at(k, r + 1), source_at(k, r), scale_at(r))
            if r < 7:
                v1[k, r - 5] = value
            else:
                v1_more[k, r - 7] = value

    def v1_at(k, r):
        return v1[k, r - 5] if r < 7 else v1_more[k, r - 7]

    for r in range(6, 10):
        for k in range(COMP):
            value = relaxed_row(v1_at(k, r), v1_at(k, r - 1), v1_at(k, r + 1), source_at(k, r), scale_at(r))
            if r < 8:
                w2[k, r - 6] = value
            else:
                w2_more[k, r - 8] = value

    def w2_at(k, r):
        return w2[k, r - 6] if r < 8 else w2_more[k, r - 8]

    for r in range(6, 9):

        def read(k, at, r=r):
            return w2[k, r - 6, at] if r < 8 else w2_more[k, r - 8, at]

        def write_source(k, at, value, r=r):
            if r < 8:
                source2[k, r - 6, at] = value
            else:
                near_source[k, 0, at] = value

        def write_scale(at, value, r=r):
            if r < 8:
                scale2[r - 6, at] = value
            else:
                near_scale[0, at] = value

        bulk_row(read, write_source, write_scale, count, cross)
    for r in range(7, 9):
        for k in range(COMP):
            src = source2[k, r - 6] if r < 8 else near_source[k, 0]
            scl = scale2[r - 6] if r < 8 else near_scale[0]
            v2[k, r - 7] = relaxed_row(w2_at(k, r), w2_at(k, r - 1), w2_at(k, r + 1), src, scl)


def far_rows(outer, inner, far, source, scale, v1, w2, source2, scale2, v2, work, emit):
    wf, far_source, far_scale, v1_far, w2_far, source2_far, scale2_far, v2_far = work
    row = row_of()
    count = outer.shape[2]
    index = index_in_space()
    edge = (index == 0) | (index == lax.axis_size("outer") * lax.axis_size("inner") - 1)
    masked = jnp.where(edge, 0.0, cross)
    for j in range(ROWS):
        for k in range(COMP):
            wf[k, j] = spaced(far, k, row(j))
    for r in range(1, 4):

        def write_source(k, at, value, r=r):
            far_source[k, r - 1, at] = value

        def write_scale(at, value, r=r):
            far_scale[r - 1, at] = value

        bulk_row(lambda k, at, r=r: wf[k, r, at], write_source, write_scale, count, masked)

    def w_at(k, r):
        return wf[k, r] if r < 4 else (outer if r < 6 else inner)[k, r % 2]

    def source_at(k, r):
        return far_source[k, r - 1] if r < 4 else source[k, r - 4]

    def scale_at(r):
        return far_scale[r - 1] if r < 4 else scale[r - 4]

    for r in range(1, 5):
        for k in range(COMP):
            v1_far[k, r - 1] = relaxed_row(w_at(k, r), w_at(k, r - 1), w_at(k, r + 1), source_at(k, r), scale_at(r))

    def v1_at(k, r):
        return v1_far[k, r - 1] if r < 5 else v1[k, r - 5]

    for r in range(2, 6):
        for k in range(COMP):
            w2_far[k, r - 2] = relaxed_row(v1_at(k, r), v1_at(k, r - 1), v1_at(k, r + 1), source_at(k, r), scale_at(r))
    for r in range(3, 6):

        def write_source(k, at, value, r=r):
            source2_far[k, r - 3, at] = value

        def write_scale(at, value, r=r):
            scale2_far[r - 3, at] = value

        bulk_row(
            lambda k, at, r=r: w2_far[k, r - 2, at], write_source, write_scale, count, masked if r < 4 else cross
        )

    def w2_at(k, r):
        return w2_far[k, r - 2] if r < 6 else w2[k, r - 6]

    def source2_at(k, r):
        return source2_far[k, r - 3] if r < 6 else source2[k, r - 6]

    def scale2_at(r):
        return scale2_far[r - 3] if r < 6 else scale2[r - 6]

    for r in range(3, 7):
        for k in range(COMP):
            v2_far[k, r - 3] = relaxed_row(
                w2_at(k, r), w2_at(k, r - 1), w2_at(k, r + 1), source2_at(k, r), scale2_at(r)
            )

    def v2_at(k, r):
        return v2_far[k, r - 3] if r < 7 else v2[k, r - 7]

    for r in range(4, 8):
        for k in range(COMP):
            value = relaxed_row(v2_at(k, r), v2_at(k, r - 1), v2_at(k, r + 1), source2_at(k, r), scale2_at(r))
            emit(k, row(r - 4), value)


def store_spaced(out, k, row, value):
    count = value.shape[0]
    for v in range(count):
        out[k, row, pl.ds(v, SUB, stride=count), :] = value[v]


def far_kernel(outer, inner, far, source, scale, v1, w2, source2, scale2, v2, out, *work):
    def emit(k, row, value):
        store_spaced(out, k, row, value)

    far_rows(outer, inner, far, source, scale, v1, w2, source2, scale2, v2, work, emit)


def far_again_kernel(outer, inner, far, source, scale, v1, w2, source2, scale2, v2, rest, weights, out, share, *work):
    nz = out.shape[3]
    total = [jnp.zeros((SUB, nz), jnp.float32) for _ in range(COMP)]

    def emit(k, row, value):
        store_spaced(out, k, row, value)
        total[k] = total[k] + jnp.sum(value, axis=0)

    far_rows(outer, inner, far, source, scale, v1, w2, source2, scale2, v2, work, emit)
    again = packed_sums([jnp.sum(t, axis=0, keepdims=True) for t in total])
    value = weights[lax.axis_index("tm"), 0] * again + rest[...]
    for i in range(share.shape[0]):
        share[i] = value


def relay_kernel(parts, share):
    value = parts[0]
    for i in range(1, parts.shape[0]):
        value = value + parts[i]
    sub = lax.broadcasted_iota(jnp.int32, value.shape, 0)
    slabs = SUB // 2
    each = share.shape[0] // slabs
    for p in range(slabs):
        pair = jnp.where(sub % 2 == 0, value[2 * p : 2 * p + 1], value[2 * p + 1 : 2 * p + 2])
        for i in range(0, each, SUB):
            share[pl.ds(p * each + i, SUB), :] = pair


def residual_kernel(relaxed, again, residual, written):
    written[...] = jnp.zeros_like(written)
    slab = lax.axis_index("tm")
    for k in range(COMP):
        mine = relaxed[k]
        residual[0, k] = jnp.where(slab == 0, mine, again[k]) - mine


def correct_kernel(parts, relaxed, written, corrected):
    del written
    value = parts[pl.ds(0, SUB), :]
    for i in range(SUB, parts.shape[0], SUB):
        value = value + parts[pl.ds(i, SUB), :]
    value = value + pltpu.roll(value, 4, 0)
    value = value + pltpu.roll(value, 2, 0)
    nz = value.shape[1]
    lane = lax.broadcasted_iota(jnp.int32, value.shape, 1)
    for k in range(COMP):
        spread = jnp.take_along_axis(value, (k % BLK) * (nz // BLK) + lane // BLK, axis=1)
        which = k // BLK
        corrected[0, k] = relaxed[k] + spread[which : which + 1][None]


def slot_weights(slabs, nz, cells):
    decay = 1.0 / (1.0 + STEPS_SLAB * time_step * linear_rate)
    table = np.zeros((slabs, 3, SUB, nz))
    for own in range(slabs):
        chain = (own + 1) % slabs
        slots = {2: (own, -1.0)}
        if chain + 1 < slabs:
            slots[0] = (chain + 1, 1.0)
        if chain == 0:
            slots[1] = (0, 1.0)
        for which, (slot, sign) in slots.items():
            for target in range(slot, slabs):
                table[own, which, 2 * target : 2 * target + 2] = sign * decay ** (target - slot) / cells
    return jnp.asarray(table, jnp.float32)


def f32(*shape):
    return jax.ShapeDtypeStruct(shape, jnp.float32)


def call(kernel, name, out, inputs, scratch=()):
    vmem = pl.BlockSpec(memory_space=pltpu.VMEM)
    return pl.pallas_call(
        kernel,
        out_shape=out,
        in_specs=[vmem] * len(inputs),
        out_specs=jax.tree.map(lambda _: vmem, out),
        scratch_shapes=list(scratch),
        compiler_params=LIMIT,
        name=name,
    )(*inputs)


def per_device(q_start, guess):
    own = guess[0]
    slabs = lax.axis_size("tm")
    count = lax.axis_size("outer") * lax.axis_size("inner")
    _, rows, ny, nz = own.shape
    row = (ny // SUB, SUB, nz)
    near_pairs = [(i, i ^ 1) for i in range(count)]
    far_pairs = []
    for i in range(1, count - 1, 2):
        far_pairs += [(i, i + 1), (i + 1, i)]

    def several(*lead):
        return f32(*lead, *row)

    def scratch(*lead):
        return pltpu.VMEM((*lead, *row), jnp.float32)

    prepared = (several(COMP, 2), several(COMP, 2), several(COMP, ROWS), several(ROWS))
    state = (several(COMP, 2), several(COMP, 2), several(COMP, 2), several(2), several(COMP, 2))
    near_scratch = (scratch(COMP, 3), scratch(3), scratch(COMP, 4), scratch(COMP, 2))
    far_scratch = (
        scratch(COMP, ROWS),
        scratch(COMP, 3),
        scratch(3),
        scratch(COMP, 4),
        scratch(COMP, 4),
        scratch(COMP, 3),
        scratch(3),
        scratch(COMP, 4),
    )

    start = jnp.where(lax.axis_index("tm") == slabs - 1, q_start, own)
    far = lax.ppermute(start, SPACE, far_pairs)
    outer, inner, source, scale = call(prepare_kernel, "prepare", prepared, (start,))
    near = [lax.ppermute(half, SPACE, near_pairs) for half in (outer, inner)]
    kept = call(near_kernel, "near", state, (outer, inner, *near, source, scale), near_scratch)
    relaxed = call(far_kernel, "far", f32(*own.shape), (outer, inner, far, source, scale, *kept), far_scratch)

    far = lax.ppermute(relaxed, SPACE, far_pairs)
    my_relaxed = lax.ppermute(relaxed, "tm", [(i, (i + 1) % slabs) for i in range(slabs)])
    weights = slot_weights(slabs, nz, count * rows * ny * BLK)
    outer, inner, source, scale, rest = call(
        prepare_again_kernel, "prepare_again", (*prepared, f32(SUB, nz)), (relaxed, guess, weights)
    )
    near = [lax.ppermute(half, SPACE, near_pairs) for half in (outer, inner)]
    kept = call(near_kernel, "near", state, (outer, inner, *near, source, scale), near_scratch)
    again, share = call(
        far_again_kernel,
        "far_again",
        (f32(*own.shape), f32(GROUP, SUB, nz)),
        (outer, inner, far, source, scale, *kept, rest, weights),
        far_scratch,
    )

    my_again = lax.ppermute(again, "tm", [(i, (i + 2) % slabs) for i in range(slabs)])
    parts = lax.all_to_all(share, "inner", 0, 0)
    wide = slabs * lax.axis_size("outer")
    share = call(relay_kernel, "relay", f32(2 * wide, nz), (parts,))
    parts = lax.all_to_all(share.reshape(wide, 2, nz), ("tm", "outer"), 0, 0).reshape(2 * wide, nz)
    residual, written = call(
        residual_kernel, "residual", (f32(1, *own.shape), f32(SUB, nz)), (my_relaxed, my_again)
    )
    corrected = call(correct_kernel, "correct", f32(1, *own.shape), (parts, my_relaxed, written))
    return corrected, residual


def solution(mesh):
    slabs, count = mesh.shape["tm"], mesh.shape["space"]
    fine = Mesh(mesh.devices.reshape(slabs, count // GROUP, GROUP), ("tm", *SPACE))
    q_spec = P(None, SPACE, None, None)
    field_spec = P("tm", None, SPACE, None, None)
    return jax.shard_map(
        per_device,
        mesh=fine,
        in_specs=(q_spec, field_spec),
        out_specs=(field_spec, field_spec),
        check_vma=False,
    )
```

```python
import jax
import jax.numpy as jnp
import numpy as np
from jax import lax
from jax.experimental import pallas as pl
from jax.experimental.pallas import tpu as pltpu
from jax.sharding import Mesh
from jax.sharding import PartitionSpec as P

COMP = 5
STEPS_SLAB = 2
BLK = 4
ROWS = 4
SUB = 8
GROUP = 16

time_step = 0.1
cross = 8.0
axial = 2.0
linear_rate = 0.1
quadratic_rate = 0.5
cubic_rate = 1.0

SPACE = ("outer", "inner")
LIMIT = pltpu.CompilerParams(vmem_limit_bytes=16 * 1024 * 1024)

LONG = pl.CostEstimate(flops=40000000000, bytes_accessed=147600000, transcendentals=0)


def index_in_space():
    return lax.axis_index("outer") * lax.axis_size("inner") + lax.axis_index("inner")


def row_of():
    odd = index_in_space() % 2 == 1
    return lambda i: jnp.where(odd, ROWS - 1 - i, i)


def spaced(ref, k, row):
    count = ref.shape[2] // SUB
    return jnp.stack([ref[k, row, pl.ds(v, SUB, stride=count), :] for v in range(count)])


def bulk(q, scale):
    a, b, c, d, e = q
    f = a + d
    aa, bb, cc, dd, ee = a * a, b * b, c * c, d * d, e * e
    off = bb + cc
    trace = aa + dd + f * f + 2.0 * (off + ee)
    third = trace * (1.0 / 3.0)
    quad = (aa + off - third, b * f + c * e, b * e - c * d, bb + dd + ee - third, b * c - a * e)
    source = [(1.0 / cross) * q[k] + (time_step * quadratic_rate / cross) * quad[k] for k in range(COMP)]
    constant = 1.0 + time_step * linear_rate + 2.0 * (2.0 * cross + axial)
    return source, scale / (constant + (time_step * cubic_rate) * trace)


def bulk_row(read, write_source, write_scale, count, scale):
    part = 2
    for v in range(0, count, part):
        at = pl.ds(v, part)
        source, ratio = bulk([read(k, at) for k in range(COMP)], scale)
        for k in range(COMP):
            write_source(k, at, source[k])
        write_scale(at, ratio)


def relaxed_row(here, low, high, source, scale):
    count, sub, nz = here.shape
    lane_of = lax.broadcasted_iota(jnp.int32, (sub, nz), 0)
    before = jnp.where(lane_of == 0, 0.0, pltpu.roll(here[count - 1], 1, 0))
    after = jnp.where(lane_of == sub - 1, 0.0, pltpu.roll(here[0], sub - 1, 0))
    along_y = jnp.concatenate([before[None], here[:-1]], axis=0) + jnp.concatenate([here[1:], after[None]], axis=0)
    along_z = pltpu.roll(here, 1, 2) + pltpu.roll(here, nz - 1, 2)
    return (source + ((low + high) + along_y) + (axial / cross) * along_z) * scale


def prepare_rows(own, packed, source, scale):
    row = row_of()
    for i in range(ROWS):
        half, j = packed[i // 2], i % 2
        for k in range(COMP):
            half[k, j] = spaced(own, k, row(i))

        def write_source(k, at, value, i=i):
            source[k, i, at] = value

        def write_scale(at, value, i=i):
            scale[i, at] = value

        def read(k, at, half=half, j=j):
            return half[k, j, at]

        bulk_row(read, write_source, write_scale, half.shape[2], cross)


def prepare_kernel(own, outer, inner, source, scale):
    prepare_rows(own, (outer, inner), source, scale)


def packed_sums(rows):
    nz = rows[0].shape[1]
    value = jnp.concatenate(rows + [jnp.zeros((SUB - COMP, nz), jnp.float32)], axis=0)
    total = value
    for i in range(1, BLK):
        total = total + pltpu.roll(value, nz - i, 1)
    blocks = nz // BLK
    lane = lax.broadcasted_iota(jnp.int32, (SUB, nz), 1)
    sub = lax.broadcasted_iota(jnp.int32, (SUB, nz), 0)
    total = jnp.take_along_axis(total, BLK * (lane % blocks), axis=1)
    first = jnp.sum(jnp.where(lane // blocks == sub, total, 0.0)[:BLK], axis=0, keepdims=True)
    second = jnp.where(lane[:1] < blocks, total[COMP - 1 : COMP], 0.0)
    return jnp.where(sub % 2 == 0, first, second)


def field_sums(field):
    return [jnp.sum(jnp.sum(field(k), axis=0), axis=0, keepdims=True) for k in range(COMP)]


def prepare_again_kernel(own, guess, weights, outer, inner, source, scale, rest):
    prepare_rows(own, (outer, inner), source, scale)
    slab = lax.axis_index("tm")
    relaxed = packed_sums(field_sums(lambda k: own[k]))
    old = packed_sums(field_sums(lambda k: guess[0, k]))
    rest[...] = weights[slab, 1] * relaxed + weights[slab, 2] * old


def near_kernel(outer, inner, near_outer, near_inner, source, scale, v1, w2, source2, scale2, v2, near_source, near_scale, v1_more, w2_more):
    count = outer.shape[2]

    def w_at(k, r, at=slice(None)):
        if r < 8:
            return (outer if r < 6 else inner)[k, r % 2, at]
        r = 11 - r
        return (near_outer if r < 2 else near_inner)[k, r % 2, at]

    for i in range(3):

        def write_source(k, at, value, i=i):
            near_source[k, i, at] = value

        def write_scale(at, value, i=i):
            near_scale[i, at] = value

        bulk_row(lambda k, at, i=i: w_at(k, 8 + i, at), write_source, write_scale, count, cross)

    def source_at(k, r):
        return source[k, r - 4] if r < 8 else near_source[k, r - 8]

    def scale_at(r):
        return scale[r - 4] if r < 8 else near_scale[r - 8]

    for r in range(5, 11):
        for k in range(COMP):
            value = relaxed_row(w_at(k, r), w_at(k, r - 1), w_at(k, r + 1), source_at(k, r), scale_at(r))
            if r < 7:
                v1[k, r - 5] = value
            else:
                v1_more[k, r - 7] = value

    def v1_at(k, r):
        return v1[k, r - 5] if r < 7 else v1_more[k, r - 7]

    for r in range(6, 10):
        for k in range(COMP):
            value = relaxed_row(v1_at(k, r), v1_at(k, r - 1), v1_at(k, r + 1), source_at(k, r), scale_at(r))
            if r < 8:
                w2[k, r - 6] = value
            else:
                w2_more[k, r - 8] = value

    def w2_at(k, r):
        return w2[k, r - 6] if r < 8 else w2_more[k, r - 8]

    for r in range(6, 9):

        def read(k, at, r=r):
            return w2[k, r - 6, at] if r < 8 else w2_more[k, r - 8, at]

        def write_source(k, at, value, r=r):
            if r < 8:
                source2[k, r - 6, at] = value
            else:
                near_source[k, 0, at] = value

        def write_scale(at, value, r=r):
            if r < 8:
                scale2[r - 6, at] = value
            else:
                near_scale[0, at] = value

        bulk_row(read, write_source, write_scale, count, cross)
    for r in range(7, 9):
        for k in range(COMP):
            src = source2[k, r - 6] if r < 8 else near_source[k, 0]
            scl = scale2[r - 6] if r < 8 else near_scale[0]
            v2[k, r - 7] = relaxed_row(w2_at(k, r), w2_at(k, r - 1), w2_at(k, r + 1), src, scl)


def far_rows(outer, inner, far, source, scale, v1, w2, source2, scale2, v2, work, emit):
    wf, far_source, far_scale, v1_far, w2_far, source2_far, scale2_far, v2_far = work
    row = row_of()
    count = outer.shape[2]
    index = index_in_space()
    edge = (index == 0) | (index == lax.axis_size("outer") * lax.axis_size("inner") - 1)
    masked = jnp.where(edge, 0.0, cross)
    for j in range(ROWS):
        for k in range(COMP):
            wf[k, j] = spaced(far, k, row(j))
    for r in range(1, 4):

        def write_source(k, at, value, r=r):
            far_source[k, r - 1, at] = value

        def write_scale(at, value, r=r):
            far_scale[r - 1, at] = value

        bulk_row(lambda k, at, r=r: wf[k, r, at], write_source, write_scale, count, masked)

    def w_at(k, r):
        return wf[k, r] if r < 4 else (outer if r < 6 else inner)[k, r % 2]

    def source_at(k, r):
        return far_source[k, r - 1] if r < 4 else source[k, r - 4]

    def scale_at(r):
        return far_scale[r - 1] if r < 4 else scale[r - 4]

    for r in range(1, 5):
        for k in range(COMP):
            v1_far[k, r - 1] = relaxed_row(w_at(k, r), w_at(k, r - 1), w_at(k, r + 1), source_at(k, r), scale_at(r))

    def v1_at(k, r):
        return v1_far[k, r - 1] if r < 5 else v1[k, r - 5]

    for r in range(2, 6):
        for k in range(COMP):
            w2_far[k, r - 2] = relaxed_row(v1_at(k, r), v1_at(k, r - 1), v1_at(k, r + 1), source_at(k, r), scale_at(r))
    for r in range(3, 6):

        def write_source(k, at, value, r=r):
            source2_far[k, r - 3, at] = value

        def write_scale(at, value, r=r):
            scale2_far[r - 3, at] = value

        bulk_row(
            lambda k, at, r=r: w2_far[k, r - 2, at], write_source, write_scale, count, masked if r < 4 else cross
        )

    def w2_at(k, r):
        return w2_far[k, r - 2] if r < 6 else w2[k, r - 6]

    def source2_at(k, r):
        return source2_far[k, r - 3] if r < 6 else source2[k, r - 6]

    def scale2_at(r):
        return scale2_far[r - 3] if r < 6 else scale2[r - 6]

    for r in range(3, 7):
        for k in range(COMP):
            v2_far[k, r - 3] = relaxed_row(
                w2_at(k, r), w2_at(k, r - 1), w2_at(k, r + 1), source2_at(k, r), scale2_at(r)
            )

    def v2_at(k, r):
        return v2_far[k, r - 3] if r < 7 else v2[k, r - 7]

    for r in range(4, 8):
        for k in range(COMP):
            value = relaxed_row(v2_at(k, r), v2_at(k, r - 1), v2_at(k, r + 1), source2_at(k, r), scale2_at(r))
            emit(k, row(r - 4), value)


def store_spaced(out, k, row, value):
    count = value.shape[0]
    for v in range(count):
        out[k, row, pl.ds(v, SUB, stride=count), :] = value[v]


def far_kernel(outer, inner, far, source, scale, v1, w2, source2, scale2, v2, out, *work):
    def emit(k, row, value):
        store_spaced(out, k, row, value)

    far_rows(outer, inner, far, source, scale, v1, w2, source2, scale2, v2, work, emit)


def far_again_kernel(outer, inner, far, source, scale, v1, w2, source2, scale2, v2, rest, weights, out, share, *work):
    nz = out.shape[3]
    total = [jnp.zeros((SUB, nz), jnp.float32) for _ in range(COMP)]

    def emit(k, row, value):
        store_spaced(out, k, row, value)
        total[k] = total[k] + jnp.sum(value, axis=0)

    far_rows(outer, inner, far, source, scale, v1, w2, source2, scale2, v2, work, emit)
    again = packed_sums([jnp.sum(t, axis=0, keepdims=True) for t in total])
    value = weights[lax.axis_index("tm"), 0] * again + rest[...]
    for i in range(share.shape[0]):
        share[i] = value


def relay_kernel(parts, relaxed, share):
    del relaxed
    value = parts[0]
    for i in range(1, parts.shape[0]):
        value = value + parts[i]
    sub = lax.broadcasted_iota(jnp.int32, value.shape, 0)
    slabs = SUB // 2
    each = share.shape[0] // slabs
    for p in range(slabs):
        pair = jnp.where(sub % 2 == 0, value[2 * p : 2 * p + 1], value[2 * p + 1 : 2 * p + 2])
        for i in range(0, each, SUB):
            share[pl.ds(p * each + i, SUB), :] = pair


def residual_kernel(relaxed, again, residual, written):
    written[...] = jnp.zeros_like(written)
    slab = lax.axis_index("tm")
    for k in range(COMP):
        mine = relaxed[k]
        residual[0, k] = jnp.where(slab == 0, mine, again[k]) - mine


def correct_kernel(parts, relaxed, written, corrected):
    del written
    value = parts[pl.ds(0, SUB), :]
    for i in range(SUB, parts.shape[0], SUB):
        value = value + parts[pl.ds(i, SUB), :]
    value = value + pltpu.roll(value, 4, 0)
    value = value + pltpu.roll(value, 2, 0)
    nz = value.shape[1]
    lane = lax.broadcasted_iota(jnp.int32, value.shape, 1)
    for k in range(COMP):
        spread = jnp.take_along_axis(value, (k % BLK) * (nz // BLK) + lane // BLK, axis=1)
        which = k // BLK
        corrected[0, k] = relaxed[k] + spread[which : which + 1][None]


def slot_weights(slabs, nz, cells):
    decay = 1.0 / (1.0 + STEPS_SLAB * time_step * linear_rate)
    table = np.zeros((slabs, 3, SUB, nz))
    for own in range(slabs):
        chain = (own + 1) % slabs
        slots = {2: (own, -1.0)}
        if chain + 1 < slabs:
            slots[0] = (chain + 1, 1.0)
        if chain == 0:
            slots[1] = (0, 1.0)
        for which, (slot, sign) in slots.items():
            for target in range(slot, slabs):
                table[own, which, 2 * target : 2 * target + 2] = sign * decay ** (target - slot) / cells
    return jnp.asarray(table, jnp.float32)


def f32(*shape):
    return jax.ShapeDtypeStruct(shape, jnp.float32)


def call(kernel, name, out, inputs, scratch=(), cost=None):
    vmem = pl.BlockSpec(memory_space=pltpu.VMEM)
    return pl.pallas_call(
        kernel,
        out_shape=out,
        in_specs=[vmem] * len(inputs),
        out_specs=jax.tree.map(lambda _: vmem, out),
        scratch_shapes=list(scratch),
        compiler_params=LIMIT,
        name=name,
        cost_estimate=cost,
    )(*inputs)


def per_device(q_start, guess):
    own = guess[0]
    slabs = lax.axis_size("tm")
    count = lax.axis_size("outer") * lax.axis_size("inner")
    _, rows, ny, nz = own.shape
    row = (ny // SUB, SUB, nz)
    near_pairs = [(i, i ^ 1) for i in range(count)]
    far_pairs = []
    for i in range(1, count - 1, 2):
        far_pairs += [(i, i + 1), (i + 1, i)]

    def several(*lead):
        return f32(*lead, *row)

    def scratch(*lead):
        return pltpu.VMEM((*lead, *row), jnp.float32)

    prepared = (several(COMP, 2), several(COMP, 2), several(COMP, ROWS), several(ROWS))
    state = (several(COMP, 2), several(COMP, 2), several(COMP, 2), several(2), several(COMP, 2))
    near_scratch = (scratch(COMP, 3), scratch(3), scratch(COMP, 4), scratch(COMP, 2))
    far_scratch = (
        scratch(COMP, ROWS),
        scratch(COMP, 3),
        scratch(3),
        scratch(COMP, 4),
        scratch(COMP, 4),
        scratch(COMP, 3),
        scratch(3),
        scratch(COMP, 4),
    )

    start = jnp.where(lax.axis_index("tm") == slabs - 1, q_start, own)
    far = lax.ppermute(start, SPACE, far_pairs)
    outer, inner, source, scale = call(prepare_kernel, "prepare", prepared, (start,))
    near = [lax.ppermute(half, SPACE, near_pairs) for half in (outer, inner)]
    kept = call(near_kernel, "near", state, (outer, inner, *near, source, scale), near_scratch)
    relaxed = call(far_kernel, "far", f32(*own.shape), (outer, inner, far, source, scale, *kept), far_scratch)

    far = lax.ppermute(relaxed, SPACE, far_pairs)
    my_relaxed = lax.ppermute(relaxed, "tm", [(i, (i + 1) % slabs) for i in range(slabs)])
    weights = slot_weights(slabs, nz, count * rows * ny * BLK)
    outer, inner, source, scale, rest = call(
        prepare_again_kernel, "prepare_again", (*prepared, f32(SUB, nz)), (relaxed, guess, weights)
    )
    near = [lax.ppermute(half, SPACE, near_pairs) for half in (outer, inner)]
    kept = call(near_kernel, "near", state, (outer, inner, *near, source, scale), near_scratch)
    again, share = call(
        far_again_kernel,
        "far_again",
        (f32(*own.shape), f32(GROUP, SUB, nz)),
        (outer, inner, far, source, scale, *kept, rest, weights),
        far_scratch,
    )

    my_again = lax.ppermute(again, "tm", [(i, (i + 2) % slabs) for i in range(slabs)])
    parts = lax.all_to_all(share, "inner", 0, 0)
    wide = slabs * lax.axis_size("outer")
    share = call(relay_kernel, "relay", f32(2 * wide, nz), (parts, my_relaxed), (), LONG)
    parts = lax.all_to_all(share.reshape(wide, 2, nz), ("tm", "outer"), 0, 0).reshape(2 * wide, nz)
    residual, written = call(
        residual_kernel, "residual", (f32(1, *own.shape), f32(SUB, nz)), (my_relaxed, my_again)
    )
    corrected = call(correct_kernel, "correct", f32(1, *own.shape), (parts, my_relaxed, written))
    return corrected, residual


def solution(mesh):
    slabs, count = mesh.shape["tm"], mesh.shape["space"]
    fine = Mesh(mesh.devices.reshape(slabs, count // GROUP, GROUP), ("tm", *SPACE))
    q_spec = P(None, SPACE, None, None)
    field_spec = P("tm", None, SPACE, None, None)
    return jax.shard_map(
        per_device,
        mesh=fine,
        in_specs=(q_spec, field_spec),
        out_specs=(field_spec, field_spec),
        check_vma=False,
    )
```

```python
import jax
import jax.numpy as jnp
import numpy as np
from jax import lax
from jax.experimental import pallas as pl
from jax.experimental.pallas import tpu as pltpu
from jax.sharding import Mesh
from jax.sharding import PartitionSpec as P

COMP = 5
STEPS_SLAB = 2
BLK = 4
ROWS = 4
SUB = 8
GROUP = 16

time_step = 0.1
cross = 8.0
axial = 2.0
linear_rate = 0.1
quadratic_rate = 0.5
cubic_rate = 1.0

SPACE = ("outer", "inner")
LIMIT = pltpu.CompilerParams(vmem_limit_bytes=16 * 1024 * 1024)

SHORT = pl.CostEstimate(flops=0, bytes_accessed=0, transcendentals=0)
LONG = pl.CostEstimate(flops=40000000000, bytes_accessed=147600000, transcendentals=0)


def index_in_space():
    return lax.axis_index("outer") * lax.axis_size("inner") + lax.axis_index("inner")


def row_of():
    odd = index_in_space() % 2 == 1
    return lambda i: jnp.where(odd, ROWS - 1 - i, i)


def spaced(ref, k, row):
    count = ref.shape[2] // SUB
    return jnp.stack([ref[k, row, pl.ds(v, SUB, stride=count), :] for v in range(count)])


def bulk(q, scale):
    a, b, c, d, e = q
    f = a + d
    aa, bb, cc, dd, ee = a * a, b * b, c * c, d * d, e * e
    off = bb + cc
    trace = aa + dd + f * f + 2.0 * (off + ee)
    third = trace * (1.0 / 3.0)
    quad = (aa + off - third, b * f + c * e, b * e - c * d, bb + dd + ee - third, b * c - a * e)
    source = [(1.0 / cross) * q[k] + (time_step * quadratic_rate / cross) * quad[k] for k in range(COMP)]
    constant = 1.0 + time_step * linear_rate + 2.0 * (2.0 * cross + axial)
    return source, scale / (constant + (time_step * cubic_rate) * trace)


def bulk_row(read, write_source, write_scale, count, scale):
    part = 2
    for v in range(0, count, part):
        at = pl.ds(v, part)
        source, ratio = bulk([read(k, at) for k in range(COMP)], scale)
        for k in range(COMP):
            write_source(k, at, source[k])
        write_scale(at, ratio)


def relaxed_row(here, low, high, source, scale):
    count, sub, nz = here.shape
    lane_of = lax.broadcasted_iota(jnp.int32, (sub, nz), 0)
    before = jnp.where(lane_of == 0, 0.0, pltpu.roll(here[count - 1], 1, 0))
    after = jnp.where(lane_of == sub - 1, 0.0, pltpu.roll(here[0], sub - 1, 0))
    along_y = jnp.concatenate([before[None], here[:-1]], axis=0) + jnp.concatenate([here[1:], after[None]], axis=0)
    along_z = pltpu.roll(here, 1, 2) + pltpu.roll(here, nz - 1, 2)
    return (source + ((low + high) + along_y) + (axial / cross) * along_z) * scale


def prepare_rows(own, packed, source, scale):
    row = row_of()
    for i in range(ROWS):
        half, j = packed[i // 2], i % 2
        for k in range(COMP):
            half[k, j] = spaced(own, k, row(i))

        def write_source(k, at, value, i=i):
            source[k, i, at] = value

        def write_scale(at, value, i=i):
            scale[i, at] = value

        def read(k, at, half=half, j=j):
            return half[k, j, at]

        bulk_row(read, write_source, write_scale, half.shape[2], cross)


def prepare_kernel(own, outer, inner, source, scale):
    prepare_rows(own, (outer, inner), source, scale)


def packed_sums(rows):
    nz = rows[0].shape[1]
    value = jnp.concatenate(rows + [jnp.zeros((SUB - COMP, nz), jnp.float32)], axis=0)
    total = value
    for i in range(1, BLK):
        total = total + pltpu.roll(value, nz - i, 1)
    blocks = nz // BLK
    lane = lax.broadcasted_iota(jnp.int32, (SUB, nz), 1)
    sub = lax.broadcasted_iota(jnp.int32, (SUB, nz), 0)
    total = jnp.take_along_axis(total, BLK * (lane % blocks), axis=1)
    first = jnp.sum(jnp.where(lane // blocks == sub, total, 0.0)[:BLK], axis=0, keepdims=True)
    second = jnp.where(lane[:1] < blocks, total[COMP - 1 : COMP], 0.0)
    return jnp.where(sub % 2 == 0, first, second)


def field_sums(field):
    return [jnp.sum(jnp.sum(field(k), axis=0), axis=0, keepdims=True) for k in range(COMP)]


def prepare_again_kernel(own, guess, weights, outer, inner, source, scale, rest):
    prepare_rows(own, (outer, inner), source, scale)
    slab = lax.axis_index("tm")
    relaxed = packed_sums(field_sums(lambda k: own[k]))
    old = packed_sums(field_sums(lambda k: guess[0, k]))
    rest[...] = weights[slab, 1] * relaxed + weights[slab, 2] * old


def beyond_kernel(*refs):
    near_kernel(*refs, mirrored=False)


def near_kernel(outer, inner, near_outer, near_inner, source, scale, v1, w2, source2, scale2, v2, near_source, near_scale, v1_more, w2_more, mirrored=True):
    count = outer.shape[2]

    def w_at(k, r, at=slice(None)):
        if r < 8:
            return (outer if r < 6 else inner)[k, r % 2, at]
        r = 11 - r if mirrored else r - 8
        return (near_outer if r < 2 else near_inner)[k, r % 2, at]

    for i in range(3):

        def write_source(k, at, value, i=i):
            near_source[k, i, at] = value

        def write_scale(at, value, i=i):
            near_scale[i, at] = value

        bulk_row(lambda k, at, i=i: w_at(k, 8 + i, at), write_source, write_scale, count, cross)

    def source_at(k, r):
        return source[k, r - 4] if r < 8 else near_source[k, r - 8]

    def scale_at(r):
        return scale[r - 4] if r < 8 else near_scale[r - 8]

    for r in range(5, 11):
        for k in range(COMP):
            value = relaxed_row(w_at(k, r), w_at(k, r - 1), w_at(k, r + 1), source_at(k, r), scale_at(r))
            if r < 7:
                v1[k, r - 5] = value
            else:
                v1_more[k, r - 7] = value

    def v1_at(k, r):
        return v1[k, r - 5] if r < 7 else v1_more[k, r - 7]

    for r in range(6, 10):
        for k in range(COMP):
            value = relaxed_row(v1_at(k, r), v1_at(k, r - 1), v1_at(k, r + 1), source_at(k, r), scale_at(r))
            if r < 8:
                w2[k, r - 6] = value
            else:
                w2_more[k, r - 8] = value

    def w2_at(k, r):
        return w2[k, r - 6] if r < 8 else w2_more[k, r - 8]

    for r in range(6, 9):

        def read(k, at, r=r):
            return w2[k, r - 6, at] if r < 8 else w2_more[k, r - 8, at]

        def write_source(k, at, value, r=r):
            if r < 8:
                source2[k, r - 6, at] = value
            else:
                near_source[k, 0, at] = value

        def write_scale(at, value, r=r):
            if r < 8:
                scale2[r - 6, at] = value
            else:
                near_scale[0, at] = value

        bulk_row(read, write_source, write_scale, count, cross)
    for r in range(7, 9):
        for k in range(COMP):
            src = source2[k, r - 6] if r < 8 else near_source[k, 0]
            scl = scale2[r - 6] if r < 8 else near_scale[0]
            v2[k, r - 7] = relaxed_row(w2_at(k, r), w2_at(k, r - 1), w2_at(k, r + 1), src, scl)


def far_rows(outer, inner, far, source, scale, v1, w2, source2, scale2, v2, work, emit):
    wf, far_source, far_scale, v1_far, w2_far, source2_far, scale2_far, v2_far = work
    row = row_of()
    count = outer.shape[2]
    index = index_in_space()
    edge = (index == 0) | (index == lax.axis_size("outer") * lax.axis_size("inner") - 1)
    masked = jnp.where(edge, 0.0, cross)
    for j in range(ROWS):
        for k in range(COMP):
            wf[k, j] = jnp.where(edge, 0.0, spaced(far, k, row(j)))
    for r in range(1, 4):

        def write_source(k, at, value, r=r):
            far_source[k, r - 1, at] = value

        def write_scale(at, value, r=r):
            far_scale[r - 1, at] = value

        bulk_row(lambda k, at, r=r: wf[k, r, at], write_source, write_scale, count, masked)

    def w_at(k, r):
        return wf[k, r] if r < 4 else (outer if r < 6 else inner)[k, r % 2]

    def source_at(k, r):
        return far_source[k, r - 1] if r < 4 else source[k, r - 4]

    def scale_at(r):
        return far_scale[r - 1] if r < 4 else scale[r - 4]

    for r in range(1, 5):
        for k in range(COMP):
            v1_far[k, r - 1] = relaxed_row(w_at(k, r), w_at(k, r - 1), w_at(k, r + 1), source_at(k, r), scale_at(r))

    def v1_at(k, r):
        return v1_far[k, r - 1] if r < 5 else v1[k, r - 5]

    for r in range(2, 6):
        for k in range(COMP):
            w2_far[k, r - 2] = relaxed_row(v1_at(k, r), v1_at(k, r - 1), v1_at(k, r + 1), source_at(k, r), scale_at(r))
    for r in range(3, 6):

        def write_source(k, at, value, r=r):
            source2_far[k, r - 3, at] = value

        def write_scale(at, value, r=r):
            scale2_far[r - 3, at] = value

        bulk_row(
            lambda k, at, r=r: w2_far[k, r - 2, at], write_source, write_scale, count, masked if r < 4 else cross
        )

    def w2_at(k, r):
        return w2_far[k, r - 2] if r < 6 else w2[k, r - 6]

    def source2_at(k, r):
        return source2_far[k, r - 3] if r < 6 else source2[k, r - 6]

    def scale2_at(r):
        return scale2_far[r - 3] if r < 6 else scale2[r - 6]

    for r in range(3, 7):
        for k in range(COMP):
            v2_far[k, r - 3] = relaxed_row(
                w2_at(k, r), w2_at(k, r - 1), w2_at(k, r + 1), source2_at(k, r), scale2_at(r)
            )

    def v2_at(k, r):
        return v2_far[k, r - 3] if r < 7 else v2[k, r - 7]

    for r in range(4, 8):
        for k in range(COMP):
            value = relaxed_row(v2_at(k, r), v2_at(k, r - 1), v2_at(k, r + 1), source2_at(k, r), scale2_at(r))
            emit(k, row(r - 4), value)


def store_spaced(out, k, row, value):
    count = value.shape[0]
    for v in range(count):
        out[k, row, pl.ds(v, SUB, stride=count), :] = value[v]


def far_kernel(outer, inner, far, source, scale, v1, w2, source2, scale2, v2, out, *work):
    def emit(k, row, value):
        store_spaced(out, k, row, value)

    far_rows(outer, inner, far, source, scale, v1, w2, source2, scale2, v2, work, emit)


def far_again_kernel(outer, inner, far, source, scale, v1, w2, source2, scale2, v2, rest, weights, out, share, *work):
    nz = out.shape[3]
    total = [jnp.zeros((SUB, nz), jnp.float32) for _ in range(COMP)]

    def emit(k, row, value):
        store_spaced(out, k, row, value)
        total[k] = total[k] + jnp.sum(value, axis=0)

    far_rows(outer, inner, far, source, scale, v1, w2, source2, scale2, v2, work, emit)
    again = packed_sums([jnp.sum(t, axis=0, keepdims=True) for t in total])
    value = weights[lax.axis_index("tm"), 0] * again + rest[...]
    for i in range(share.shape[0]):
        share[i] = value


def relay_kernel(parts, relaxed, share):
    del relaxed
    value = parts[0]
    for i in range(1, parts.shape[0]):
        value = value + parts[i]
    sub = lax.broadcasted_iota(jnp.int32, value.shape, 0)
    slabs = SUB // 2
    each = share.shape[0] // slabs
    for p in range(slabs):
        pair = jnp.where(sub % 2 == 0, value[2 * p : 2 * p + 1], value[2 * p + 1 : 2 * p + 2])
        for i in range(0, each, SUB):
            share[pl.ds(p * each + i, SUB), :] = pair


def residual_kernel(relaxed, again, residual, written):
    written[...] = jnp.zeros_like(written)
    slab = lax.axis_index("tm")
    for k in range(COMP):
        mine = relaxed[k]
        residual[0, k] = jnp.where(slab == 0, mine, again[k]) - mine


def correct_kernel(parts, relaxed, written, corrected):
    del written
    value = parts[pl.ds(0, SUB), :]
    for i in range(SUB, parts.shape[0], SUB):
        value = value + parts[pl.ds(i, SUB), :]
    value = value + pltpu.roll(value, 4, 0)
    value = value + pltpu.roll(value, 2, 0)
    nz = value.shape[1]
    lane = lax.broadcasted_iota(jnp.int32, value.shape, 1)
    for k in range(COMP):
        spread = jnp.take_along_axis(value, (k % BLK) * (nz // BLK) + lane // BLK, axis=1)
        which = k // BLK
        corrected[0, k] = relaxed[k] + spread[which : which + 1][None]


def slot_weights(slabs, nz, cells):
    decay = 1.0 / (1.0 + STEPS_SLAB * time_step * linear_rate)
    table = np.zeros((slabs, 3, SUB, nz))
    for own in range(slabs):
        chain = (own + 1) % slabs
        slots = {2: (own, -1.0)}
        if chain + 1 < slabs:
            slots[0] = (chain + 1, 1.0)
        if chain == 0:
            slots[1] = (0, 1.0)
        for which, (slot, sign) in slots.items():
            for target in range(slot, slabs):
                table[own, which, 2 * target : 2 * target + 2] = sign * decay ** (target - slot) / cells
    return jnp.asarray(table, jnp.float32)


def f32(*shape):
    return jax.ShapeDtypeStruct(shape, jnp.float32)


def call(kernel, name, out, inputs, scratch=(), cost=None):
    vmem = pl.BlockSpec(memory_space=pltpu.VMEM)
    return pl.pallas_call(
        kernel,
        out_shape=out,
        in_specs=[vmem] * len(inputs),
        out_specs=jax.tree.map(lambda _: vmem, out),
        scratch_shapes=list(scratch),
        compiler_params=LIMIT,
        name=name,
        cost_estimate=cost,
    )(*inputs)


def per_device(q_start, guess):
    own = guess[0]
    slabs = lax.axis_size("tm")
    count = lax.axis_size("outer") * lax.axis_size("inner")
    _, rows, ny, nz = own.shape
    row = (ny // SUB, SUB, nz)
    near_pairs = [(i, i ^ 1) for i in range(count)]
    far_pairs = []
    for i in range(1, count - 1, 2):
        far_pairs += [(i, i + 1), (i + 1, i)]

    farther_pairs = [(i - 2, i) for i in range(2, count, 2)] + [(i + 2, i) for i in range(1, count - 2, 2)]

    def several(*lead):
        return f32(*lead, *row)

    def scratch(*lead):
        return pltpu.VMEM((*lead, *row), jnp.float32)

    prepared = (several(COMP, 2), several(COMP, 2), several(COMP, ROWS), several(ROWS))
    state = (several(COMP, 2), several(COMP, 2), several(COMP, 2), several(2), several(COMP, 2))
    near_scratch = (scratch(COMP, 3), scratch(3), scratch(COMP, 4), scratch(COMP, 2))
    far_scratch = (
        scratch(COMP, ROWS),
        scratch(COMP, 3),
        scratch(3),
        scratch(COMP, 4),
        scratch(COMP, 4),
        scratch(COMP, 3),
        scratch(3),
        scratch(COMP, 4),
    )

    start = jnp.where(lax.axis_index("tm") == slabs - 1, q_start, own)
    far = lax.ppermute(start, SPACE, far_pairs)
    outer, inner, source, scale = call(prepare_kernel, "prepare", prepared, (start,))
    near = [lax.ppermute(half, SPACE, near_pairs) for half in (outer, inner)]
    kept = call(near_kernel, "near", state, (outer, inner, *near, source, scale), near_scratch, SHORT)
    held, kept = lax.optimization_barrier((start, kept))
    farther = lax.ppermute(held, SPACE, farther_pairs)
    relaxed = call(
        far_kernel, "far", f32(*own.shape), (outer, inner, far, source, scale, *kept), far_scratch, SHORT
    )

    beyond = call(prepare_kernel, "prepare_far", prepared, (far,), (), SHORT)
    kept = call(
        beyond_kernel, "beyond", state, (*beyond[:2], outer, inner, *beyond[2:]), near_scratch, SHORT
    )
    far = call(
        far_kernel,
        "far_relaxed",
        f32(*own.shape),
        (*beyond[:2], farther, *beyond[2:], *kept),
        far_scratch,
        SHORT,
    )
    my_relaxed = lax.ppermute(relaxed, "tm", [(i, (i + 1) % slabs) for i in range(slabs)])
    weights = slot_weights(slabs, nz, count * rows * ny * BLK)
    outer, inner, source, scale, rest = call(
        prepare_again_kernel, "prepare_again", (*prepared, f32(SUB, nz)), (relaxed, guess, weights), (), SHORT
    )
    near = [lax.ppermute(half, SPACE, near_pairs) for half in (outer, inner)]
    kept = call(near_kernel, "near", state, (outer, inner, *near, source, scale), near_scratch, SHORT)
    again, share = call(
        far_again_kernel,
        "far_again",
        (f32(*own.shape), f32(GROUP, SUB, nz)),
        (outer, inner, far, source, scale, *kept, rest, weights),
        far_scratch,
    )

    my_again = lax.ppermute(again, "tm", [(i, (i + 2) % slabs) for i in range(slabs)])
    parts = lax.all_to_all(share, "inner", 0, 0)
    wide = slabs * lax.axis_size("outer")
    share = call(relay_kernel, "relay", f32(2 * wide, nz), (parts, my_relaxed), (), LONG)
    parts = lax.all_to_all(share.reshape(wide, 2, nz), ("tm", "outer"), 0, 0).reshape(2 * wide, nz)
    residual, written = call(
        residual_kernel, "residual", (f32(1, *own.shape), f32(SUB, nz)), (my_relaxed, my_again)
    )
    corrected = call(correct_kernel, "correct", f32(1, *own.shape), (parts, my_relaxed, written))
    return corrected, residual


def solution(mesh):
    slabs, count = mesh.shape["tm"], mesh.shape["space"]
    fine = Mesh(mesh.devices.reshape(slabs, count // GROUP, GROUP), ("tm", *SPACE))
    q_spec = P(None, SPACE, None, None)
    field_spec = P("tm", None, SPACE, None, None)
    return jax.shard_map(
        per_device,
        mesh=fine,
        in_specs=(q_spec, field_spec),
        out_specs=(field_spec, field_spec),
        check_vma=False,
    )
```

```python
import jax
import jax.numpy as jnp
import numpy as np
from jax import lax
from jax.experimental import pallas as pl
from jax.experimental.pallas import tpu as pltpu
from jax.sharding import Mesh
from jax.sharding import PartitionSpec as P

COMP = 5
STEPS_SLAB = 2
BLK = 4
ROWS = 4
SUB = 8
GROUP = 16

time_step = 0.1
cross = 8.0
axial = 2.0
linear_rate = 0.1
quadratic_rate = 0.5
cubic_rate = 1.0

SPACE = ("outer", "inner")
LIMIT = pltpu.CompilerParams(vmem_limit_bytes=16 * 1024 * 1024)

SHORT = pl.CostEstimate(flops=0, bytes_accessed=0, transcendentals=0)
LONG = pl.CostEstimate(flops=40000000000, bytes_accessed=147600000, transcendentals=0)


def index_in_space():
    return lax.axis_index("outer") * lax.axis_size("inner") + lax.axis_index("inner")


def row_of():
    odd = index_in_space() % 2 == 1
    return lambda i: jnp.where(odd, ROWS - 1 - i, i)


def spaced(ref, k, row):
    count = ref.shape[2] // SUB
    return jnp.stack([ref[k, row, pl.ds(v, SUB, stride=count), :] for v in range(count)])


def bulk(q, scale):
    a, b, c, d, e = q
    f = a + d
    aa, bb, cc, dd, ee = a * a, b * b, c * c, d * d, e * e
    off = bb + cc
    trace = aa + dd + f * f + 2.0 * (off + ee)
    third = trace * (1.0 / 3.0)
    quad = (aa + off - third, b * f + c * e, b * e - c * d, bb + dd + ee - third, b * c - a * e)
    source = [(1.0 / cross) * q[k] + (time_step * quadratic_rate / cross) * quad[k] for k in range(COMP)]
    constant = 1.0 + time_step * linear_rate + 2.0 * (2.0 * cross + axial)
    return source, scale / (constant + (time_step * cubic_rate) * trace)


def bulk_row(read, write_source, write_scale, count, scale):
    part = 2
    for v in range(0, count, part):
        at = pl.ds(v, part)
        source, ratio = bulk([read(k, at) for k in range(COMP)], scale)
        for k in range(COMP):
            write_source(k, at, source[k])
        write_scale(at, ratio)


def relaxed_row(here, low, high, source, scale):
    count, sub, nz = here.shape
    lane_of = lax.broadcasted_iota(jnp.int32, (sub, nz), 0)
    before = jnp.where(lane_of == 0, 0.0, pltpu.roll(here[count - 1], 1, 0))
    after = jnp.where(lane_of == sub - 1, 0.0, pltpu.roll(here[0], sub - 1, 0))
    along_y = jnp.concatenate([before[None], here[:-1]], axis=0) + jnp.concatenate([here[1:], after[None]], axis=0)
    along_z = pltpu.roll(here, 1, 2) + pltpu.roll(here, nz - 1, 2)
    return (source + ((low + high) + along_y) + (axial / cross) * along_z) * scale


def prepare_rows(own, packed, source, scale):
    row = row_of()
    for i in range(ROWS):
        half, j = packed[i // 2], i % 2
        for k in range(COMP):
            half[k, j] = spaced(own, k, row(i))

        def write_source(k, at, value, i=i):
            source[k, i, at] = value

        def write_scale(at, value, i=i):
            scale[i, at] = value

        def read(k, at, half=half, j=j):
            return half[k, j, at]

        bulk_row(read, write_source, write_scale, half.shape[2], cross)


def prepare_kernel(own, outer, inner, source, scale):
    prepare_rows(own, (outer, inner), source, scale)


def packed_sums(rows):
    nz = rows[0].shape[1]
    value = jnp.concatenate(rows + [jnp.zeros((SUB - COMP, nz), jnp.float32)], axis=0)
    total = value
    for i in range(1, BLK):
        total = total + pltpu.roll(value, nz - i, 1)
    blocks = nz // BLK
    lane = lax.broadcasted_iota(jnp.int32, (SUB, nz), 1)
    sub = lax.broadcasted_iota(jnp.int32, (SUB, nz), 0)
    total = jnp.take_along_axis(total, BLK * (lane % blocks), axis=1)
    first = jnp.sum(jnp.where(lane // blocks == sub, total, 0.0)[:BLK], axis=0, keepdims=True)
    second = jnp.where(lane[:1] < blocks, total[COMP - 1 : COMP], 0.0)
    return jnp.where(sub % 2 == 0, first, second)


def field_sums(field):
    return [jnp.sum(jnp.sum(field(k), axis=0), axis=0, keepdims=True) for k in range(COMP)]


def halves(packed):
    return packed.at[:, pl.ds(0, 2)], packed.at[:, pl.ds(2, 2)]


def prepare_again_kernel(own, guess, weights, packed, source, scale, rest):
    prepare_rows(own, halves(packed), source, scale)
    slab = lax.axis_index("tm")
    relaxed = packed_sums(field_sums(lambda k: own[k]))
    old = packed_sums(field_sums(lambda k: guess[0, k]))
    rest[...] = weights[slab, 1] * relaxed + weights[slab, 2] * old


def beyond_kernel(*refs):
    near_kernel(*refs, mirrored=False)


def near_again_kernel(packed, near, *refs):
    near_kernel(*halves(packed), *halves(near), *refs)


def near_kernel(outer, inner, near_outer, near_inner, source, scale, v1, w2, source2, scale2, v2, near_source, near_scale, v1_more, w2_more, mirrored=True):
    count = outer.shape[2]

    def w_at(k, r, at=slice(None)):
        if r < 8:
            return (outer if r < 6 else inner)[k, r % 2, at]
        r = 11 - r if mirrored else r - 8
        return (near_outer if r < 2 else near_inner)[k, r % 2, at]

    for i in range(3):

        def write_source(k, at, value, i=i):
            near_source[k, i, at] = value

        def write_scale(at, value, i=i):
            near_scale[i, at] = value

        bulk_row(lambda k, at, i=i: w_at(k, 8 + i, at), write_source, write_scale, count, cross)

    def source_at(k, r):
        return source[k, r - 4] if r < 8 else near_source[k, r - 8]

    def scale_at(r):
        return scale[r - 4] if r < 8 else near_scale[r - 8]

    for r in range(5, 11):
        for k in range(COMP):
            value = relaxed_row(w_at(k, r), w_at(k, r - 1), w_at(k, r + 1), source_at(k, r), scale_at(r))
            if r < 7:
                v1[k, r - 5] = value
            else:
                v1_more[k, r - 7] = value

    def v1_at(k, r):
        return v1[k, r - 5] if r < 7 else v1_more[k, r - 7]

    for r in range(6, 10):
        for k in range(COMP):
            value = relaxed_row(v1_at(k, r), v1_at(k, r - 1), v1_at(k, r + 1), source_at(k, r), scale_at(r))
            if r < 8:
                w2[k, r - 6] = value
            else:
                w2_more[k, r - 8] = value

    def w2_at(k, r):
        return w2[k, r - 6] if r < 8 else w2_more[k, r - 8]

    for r in range(6, 9):

        def read(k, at, r=r):
            return w2[k, r - 6, at] if r < 8 else w2_more[k, r - 8, at]

        def write_source(k, at, value, r=r):
            if r < 8:
                source2[k, r - 6, at] = value
            else:
                near_source[k, 0, at] = value

        def write_scale(at, value, r=r):
            if r < 8:
                scale2[r - 6, at] = value
            else:
                near_scale[0, at] = value

        bulk_row(read, write_source, write_scale, count, cross)
    for r in range(7, 9):
        for k in range(COMP):
            src = source2[k, r - 6] if r < 8 else near_source[k, 0]
            scl = scale2[r - 6] if r < 8 else near_scale[0]
            v2[k, r - 7] = relaxed_row(w2_at(k, r), w2_at(k, r - 1), w2_at(k, r + 1), src, scl)


def far_rows(outer, inner, far, source, scale, v1, w2, source2, scale2, v2, work, emit):
    wf, far_source, far_scale, v1_far, w2_far, source2_far, scale2_far, v2_far = work
    row = row_of()
    count = outer.shape[2]
    index = index_in_space()
    edge = (index == 0) | (index == lax.axis_size("outer") * lax.axis_size("inner") - 1)
    masked = jnp.where(edge, 0.0, cross)
    for j in range(ROWS):
        for k in range(COMP):
            wf[k, j] = jnp.where(edge, 0.0, spaced(far, k, row(j)))
    for r in range(1, 4):

        def write_source(k, at, value, r=r):
            far_source[k, r - 1, at] = value

        def write_scale(at, value, r=r):
            far_scale[r - 1, at] = value

        bulk_row(lambda k, at, r=r: wf[k, r, at], write_source, write_scale, count, masked)

    def w_at(k, r):
        return wf[k, r] if r < 4 else (outer if r < 6 else inner)[k, r % 2]

    def source_at(k, r):
        return far_source[k, r - 1] if r < 4 else source[k, r - 4]

    def scale_at(r):
        return far_scale[r - 1] if r < 4 else scale[r - 4]

    for r in range(1, 5):
        for k in range(COMP):
            v1_far[k, r - 1] = relaxed_row(w_at(k, r), w_at(k, r - 1), w_at(k, r + 1), source_at(k, r), scale_at(r))

    def v1_at(k, r):
        return v1_far[k, r - 1] if r < 5 else v1[k, r - 5]

    for r in range(2, 6):
        for k in range(COMP):
            w2_far[k, r - 2] = relaxed_row(v1_at(k, r), v1_at(k, r - 1), v1_at(k, r + 1), source_at(k, r), scale_at(r))
    for r in range(3, 6):

        def write_source(k, at, value, r=r):
            source2_far[k, r - 3, at] = value

        def write_scale(at, value, r=r):
            scale2_far[r - 3, at] = value

        bulk_row(
            lambda k, at, r=r: w2_far[k, r - 2, at], write_source, write_scale, count, masked if r < 4 else cross
        )

    def w2_at(k, r):
        return w2_far[k, r - 2] if r < 6 else w2[k, r - 6]

    def source2_at(k, r):
        return source2_far[k, r - 3] if r < 6 else source2[k, r - 6]

    def scale2_at(r):
        return scale2_far[r - 3] if r < 6 else scale2[r - 6]

    for r in range(3, 7):
        for k in range(COMP):
            v2_far[k, r - 3] = relaxed_row(
                w2_at(k, r), w2_at(k, r - 1), w2_at(k, r + 1), source2_at(k, r), scale2_at(r)
            )

    def v2_at(k, r):
        return v2_far[k, r - 3] if r < 7 else v2[k, r - 7]

    for r in range(4, 8):
        for k in range(COMP):
            value = relaxed_row(v2_at(k, r), v2_at(k, r - 1), v2_at(k, r + 1), source2_at(k, r), scale2_at(r))
            emit(k, row(r - 4), value)


def store_spaced(out, k, row, value):
    count = value.shape[0]
    for v in range(count):
        out[k, row, pl.ds(v, SUB, stride=count), :] = value[v]


def far_kernel(outer, inner, far, source, scale, v1, w2, source2, scale2, v2, out, *work):
    def emit(k, row, value):
        store_spaced(out, k, row, value)

    far_rows(outer, inner, far, source, scale, v1, w2, source2, scale2, v2, work, emit)


def far_again_kernel(packed, far, source, scale, v1, w2, source2, scale2, v2, rest, weights, out, share, *work):
    nz = out.shape[3]
    total = [jnp.zeros((SUB, nz), jnp.float32) for _ in range(COMP)]

    def emit(k, row, value):
        store_spaced(out, k, row, value)
        total[k] = total[k] + jnp.sum(value, axis=0)

    far_rows(*halves(packed), far, source, scale, v1, w2, source2, scale2, v2, work, emit)
    again = packed_sums([jnp.sum(t, axis=0, keepdims=True) for t in total])
    value = weights[lax.axis_index("tm"), 0] * again + rest[...]
    for i in range(share.shape[0]):
        share[i] = value


def relay_kernel(parts, relaxed, share):
    del relaxed
    value = parts[0]
    for i in range(1, parts.shape[0]):
        value = value + parts[i]
    sub = lax.broadcasted_iota(jnp.int32, value.shape, 0)
    slabs = SUB // 2
    each = share.shape[0] // slabs
    for p in range(slabs):
        pair = jnp.where(sub % 2 == 0, value[2 * p : 2 * p + 1], value[2 * p + 1 : 2 * p + 2])
        for i in range(0, each, SUB):
            share[pl.ds(p * each + i, SUB), :] = pair


def residual_kernel(relaxed, again, residual, written):
    written[...] = jnp.zeros_like(written)
    slab = lax.axis_index("tm")
    for k in range(COMP):
        mine = relaxed[k]
        residual[0, k] = jnp.where(slab == 0, mine, again[k]) - mine


def correct_kernel(parts, relaxed, written, corrected):
    del written
    value = parts[pl.ds(0, SUB), :]
    for i in range(SUB, parts.shape[0], SUB):
        value = value + parts[pl.ds(i, SUB), :]
    value = value + pltpu.roll(value, 4, 0)
    value = value + pltpu.roll(value, 2, 0)
    nz = value.shape[1]
    lane = lax.broadcasted_iota(jnp.int32, value.shape, 1)
    for k in range(COMP):
        spread = jnp.take_along_axis(value, (k % BLK) * (nz // BLK) + lane // BLK, axis=1)
        which = k // BLK
        corrected[0, k] = relaxed[k] + spread[which : which + 1][None]


def slot_weights(slabs, nz, cells):
    decay = 1.0 / (1.0 + STEPS_SLAB * time_step * linear_rate)
    table = np.zeros((slabs, 3, SUB, nz))
    for own in range(slabs):
        chain = (own + 1) % slabs
        slots = {2: (own, -1.0)}
        if chain + 1 < slabs:
            slots[0] = (chain + 1, 1.0)
        if chain == 0:
            slots[1] = (0, 1.0)
        for which, (slot, sign) in slots.items():
            for target in range(slot, slabs):
                table[own, which, 2 * target : 2 * target + 2] = sign * decay ** (target - slot) / cells
    return jnp.asarray(table, jnp.float32)


def f32(*shape):
    return jax.ShapeDtypeStruct(shape, jnp.float32)


def call(kernel, name, out, inputs, scratch=(), cost=None):
    vmem = pl.BlockSpec(memory_space=pltpu.VMEM)
    return pl.pallas_call(
        kernel,
        out_shape=out,
        in_specs=[vmem] * len(inputs),
        out_specs=jax.tree.map(lambda _: vmem, out),
        scratch_shapes=list(scratch),
        compiler_params=LIMIT,
        name=name,
        cost_estimate=cost,
    )(*inputs)


def per_device(q_start, guess):
    own = guess[0]
    slabs = lax.axis_size("tm")
    count = lax.axis_size("outer") * lax.axis_size("inner")
    _, rows, ny, nz = own.shape
    row = (ny // SUB, SUB, nz)
    near_pairs = [(i, i ^ 1) for i in range(count)]
    far_pairs = []
    for i in range(1, count - 1, 2):
        far_pairs += [(i, i + 1), (i + 1, i)]

    farther_pairs = [(i - 2, i) for i in range(2, count, 2)] + [(i + 2, i) for i in range(1, count - 2, 2)]

    def several(*lead):
        return f32(*lead, *row)

    def scratch(*lead):
        return pltpu.VMEM((*lead, *row), jnp.float32)

    prepared = (several(COMP, 2), several(COMP, 2), several(COMP, ROWS), several(ROWS))
    state = (several(COMP, 2), several(COMP, 2), several(COMP, 2), several(2), several(COMP, 2))
    near_scratch = (scratch(COMP, 3), scratch(3), scratch(COMP, 4), scratch(COMP, 2))
    far_scratch = (
        scratch(COMP, ROWS),
        scratch(COMP, 3),
        scratch(3),
        scratch(COMP, 4),
        scratch(COMP, 4),
        scratch(COMP, 3),
        scratch(3),
        scratch(COMP, 4),
    )

    start = jnp.where(lax.axis_index("tm") == slabs - 1, q_start, own)
    far = lax.ppermute(start, SPACE, far_pairs)
    outer, inner, source, scale = call(prepare_kernel, "prepare", prepared, (start,))
    near = [lax.ppermute(half, SPACE, near_pairs) for half in (outer, inner)]
    kept = call(near_kernel, "near", state, (outer, inner, *near, source, scale), near_scratch, SHORT)
    held, kept = lax.optimization_barrier((start, kept))
    farther = lax.ppermute(held, SPACE, farther_pairs)
    relaxed = call(
        far_kernel, "far", f32(*own.shape), (outer, inner, far, source, scale, *kept), far_scratch, SHORT
    )

    beyond = call(prepare_kernel, "prepare_far", prepared, (far,), (), SHORT)
    kept = call(
        beyond_kernel, "beyond", state, (*beyond[:2], outer, inner, *beyond[2:]), near_scratch, SHORT
    )
    far = call(
        far_kernel,
        "far_relaxed",
        f32(*own.shape),
        (*beyond[:2], farther, *beyond[2:], *kept),
        far_scratch,
        SHORT,
    )
    my_relaxed = lax.ppermute(relaxed, "tm", [(i, (i + 1) % slabs) for i in range(slabs)])
    weights = slot_weights(slabs, nz, count * rows * ny * BLK)
    packed, source, scale, rest = call(
        prepare_again_kernel,
        "prepare_again",
        (several(COMP, ROWS), *prepared[2:], f32(SUB, nz)),
        (relaxed, guess, weights),
        (),
        SHORT,
    )
    near = lax.ppermute(packed, SPACE, near_pairs)
    kept = call(
        near_again_kernel, "near_again", state, (packed, near, source, scale), near_scratch, SHORT
    )
    again, share = call(
        far_again_kernel,
        "far_again",
        (f32(*own.shape), f32(GROUP, SUB, nz)),
        (packed, far, source, scale, *kept, rest, weights),
        far_scratch,
    )

    my_again = lax.ppermute(again, "tm", [(i, (i + 2) % slabs) for i in range(slabs)])
    parts = lax.all_to_all(share, "inner", 0, 0)
    wide = slabs * lax.axis_size("outer")
    share = call(relay_kernel, "relay", f32(2 * wide, nz), (parts, my_relaxed), (), LONG)
    parts = lax.all_to_all(share.reshape(wide, 2, nz), ("tm", "outer"), 0, 0).reshape(2 * wide, nz)
    residual, written = call(
        residual_kernel, "residual", (f32(1, *own.shape), f32(SUB, nz)), (my_relaxed, my_again)
    )
    corrected = call(correct_kernel, "correct", f32(1, *own.shape), (parts, my_relaxed, written))
    return corrected, residual


def solution(mesh):
    slabs, count = mesh.shape["tm"], mesh.shape["space"]
    fine = Mesh(mesh.devices.reshape(slabs, count // GROUP, GROUP), ("tm", *SPACE))
    q_spec = P(None, SPACE, None, None)
    field_spec = P("tm", None, SPACE, None, None)
    return jax.shard_map(
        per_device,
        mesh=fine,
        in_specs=(q_spec, field_spec),
        out_specs=(field_spec, field_spec),
        check_vma=False,
    )
```

```python
import jax
import jax.numpy as jnp
import numpy as np
from jax import lax
from jax.experimental import pallas as pl
from jax.experimental.pallas import tpu as pltpu
from jax.sharding import Mesh
from jax.sharding import PartitionSpec as P

COMP = 5
STEPS_SLAB = 2
BLK = 4
ROWS = 4
SUB = 8
GROUP = 16

time_step = 0.1
cross = 8.0
axial = 2.0
linear_rate = 0.1
quadratic_rate = 0.5
cubic_rate = 1.0

SPACE = ("outer", "inner")
LIMIT = pltpu.CompilerParams(vmem_limit_bytes=16 * 1024 * 1024)

SHORT = pl.CostEstimate(flops=0, bytes_accessed=0, transcendentals=0)
LONG = pl.CostEstimate(flops=40000000000, bytes_accessed=147600000, transcendentals=0)


def index_in_space():
    return lax.axis_index("outer") * lax.axis_size("inner") + lax.axis_index("inner")


def row_of():
    odd = index_in_space() % 2 == 1
    return lambda i: jnp.where(odd, ROWS - 1 - i, i)


def spaced(ref, k, row):
    count = ref.shape[2] // SUB
    return jnp.stack([ref[k, row, pl.ds(v, SUB, stride=count), :] for v in range(count)])


def bulk(q, scale):
    a, b, c, d, e = q
    f = a + d
    aa, bb, cc, dd, ee = a * a, b * b, c * c, d * d, e * e
    off = bb + cc
    trace = aa + dd + f * f + 2.0 * (off + ee)
    third = trace * (1.0 / 3.0)
    quad = (aa + off - third, b * f + c * e, b * e - c * d, bb + dd + ee - third, b * c - a * e)
    source = [(1.0 / cross) * q[k] + (time_step * quadratic_rate / cross) * quad[k] for k in range(COMP)]
    constant = 1.0 + time_step * linear_rate + 2.0 * (2.0 * cross + axial)
    return source, scale / (constant + (time_step * cubic_rate) * trace)


def bulk_row(read, write_source, write_scale, count, scale):
    part = 2
    for v in range(0, count, part):
        at = pl.ds(v, part)
        source, ratio = bulk([read(k, at) for k in range(COMP)], scale)
        for k in range(COMP):
            write_source(k, at, source[k])
        write_scale(at, ratio)


def relaxed_row(here, low, high, source, scale):
    count, sub, nz = here.shape
    lane_of = lax.broadcasted_iota(jnp.int32, (sub, nz), 0)
    before = jnp.where(lane_of == 0, 0.0, pltpu.roll(here[count - 1], 1, 0))
    after = jnp.where(lane_of == sub - 1, 0.0, pltpu.roll(here[0], sub - 1, 0))
    along_y = jnp.concatenate([before[None], here[:-1]], axis=0) + jnp.concatenate([here[1:], after[None]], axis=0)
    along_z = pltpu.roll(here, 1, 2) + pltpu.roll(here, nz - 1, 2)
    return (source + ((low + high) + along_y) + (axial / cross) * along_z) * scale


def prepare_rows(own, packed, source, scale):
    row = row_of()
    for i in range(ROWS):
        half, j = packed[i // 2], i % 2
        for k in range(COMP):
            half[k, j] = spaced(own, k, row(i))

        def write_source(k, at, value, i=i):
            source[k, i, at] = value

        def write_scale(at, value, i=i):
            scale[i, at] = value

        def read(k, at, half=half, j=j):
            return half[k, j, at]

        bulk_row(read, write_source, write_scale, half.shape[2], cross)


def prepare_kernel(own, outer, inner, source, scale):
    prepare_rows(own, (outer, inner), source, scale)


def packed_sums(rows):
    nz = rows[0].shape[1]
    value = jnp.concatenate(rows + [jnp.zeros((SUB - COMP, nz), jnp.float32)], axis=0)
    total = value
    for i in range(1, BLK):
        total = total + pltpu.roll(value, nz - i, 1)
    blocks = nz // BLK
    lane = lax.broadcasted_iota(jnp.int32, (SUB, nz), 1)
    sub = lax.broadcasted_iota(jnp.int32, (SUB, nz), 0)
    total = jnp.take_along_axis(total, BLK * (lane % blocks), axis=1)
    first = jnp.sum(jnp.where(lane // blocks == sub, total, 0.0)[:BLK], axis=0, keepdims=True)
    second = jnp.where(lane[:1] < blocks, total[COMP - 1 : COMP], 0.0)
    return jnp.where(sub % 2 == 0, first, second)


def field_sums(field):
    return [jnp.sum(jnp.sum(field(k), axis=0), axis=0, keepdims=True) for k in range(COMP)]


def halves(packed):
    return packed.at[:, pl.ds(0, 2)], packed.at[:, pl.ds(2, 2)]


def prepare_again_kernel(own, guess, weights, packed, source, scale, rest):
    prepare_rows(own, halves(packed), source, scale)
    slab = lax.axis_index("tm")
    relaxed = packed_sums(field_sums(lambda k: own[k]))
    old = packed_sums(field_sums(lambda k: guess[0, k]))
    rest[...] = weights[slab, 1] * relaxed + weights[slab, 2] * old


def beyond_kernel(*refs):
    near_kernel(*refs, mirrored=False)


def near_again_kernel(packed, near, *refs):
    near_kernel(*halves(packed), *halves(near), *refs)


def near_kernel(outer, inner, near_outer, near_inner, source, scale, v1, w2, source2, scale2, v2, near_source, near_scale, v1_more, w2_more, mirrored=True):
    count = outer.shape[2]

    def w_at(k, r, at=slice(None)):
        if r < 8:
            return (outer if r < 6 else inner)[k, r % 2, at]
        r = 11 - r if mirrored else r - 8
        return (near_outer if r < 2 else near_inner)[k, r % 2, at]

    for i in range(3):

        def write_source(k, at, value, i=i):
            near_source[k, i, at] = value

        def write_scale(at, value, i=i):
            near_scale[i, at] = value

        bulk_row(lambda k, at, i=i: w_at(k, 8 + i, at), write_source, write_scale, count, cross)

    def source_at(k, r):
        return source[k, r - 4] if r < 8 else near_source[k, r - 8]

    def scale_at(r):
        return scale[r - 4] if r < 8 else near_scale[r - 8]

    for r in range(5, 11):
        for k in range(COMP):
            value = relaxed_row(w_at(k, r), w_at(k, r - 1), w_at(k, r + 1), source_at(k, r), scale_at(r))
            if r < 7:
                v1[k, r - 5] = value
            else:
                v1_more[k, r - 7] = value

    def v1_at(k, r):
        return v1[k, r - 5] if r < 7 else v1_more[k, r - 7]

    for r in range(6, 10):
        for k in range(COMP):
            value = relaxed_row(v1_at(k, r), v1_at(k, r - 1), v1_at(k, r + 1), source_at(k, r), scale_at(r))
            if r < 8:
                w2[k, r - 6] = value
            else:
                w2_more[k, r - 8] = value

    def w2_at(k, r):
        return w2[k, r - 6] if r < 8 else w2_more[k, r - 8]

    for r in range(6, 9):

        def read(k, at, r=r):
            return w2[k, r - 6, at] if r < 8 else w2_more[k, r - 8, at]

        def write_source(k, at, value, r=r):
            if r < 8:
                source2[k, r - 6, at] = value
            else:
                near_source[k, 0, at] = value

        def write_scale(at, value, r=r):
            if r < 8:
                scale2[r - 6, at] = value
            else:
                near_scale[0, at] = value

        bulk_row(read, write_source, write_scale, count, cross)
    for r in range(7, 9):
        for k in range(COMP):
            src = source2[k, r - 6] if r < 8 else near_source[k, 0]
            scl = scale2[r - 6] if r < 8 else near_scale[0]
            v2[k, r - 7] = relaxed_row(w2_at(k, r), w2_at(k, r - 1), w2_at(k, r + 1), src, scl)


def far_rows(outer, inner, far, source, scale, v1, w2, source2, scale2, v2, work, emit):
    wf, far_source, far_scale, v1_far, w2_far, source2_far, scale2_far, v2_far = work
    row = row_of()
    count = outer.shape[2]
    index = index_in_space()
    edge = (index == 0) | (index == lax.axis_size("outer") * lax.axis_size("inner") - 1)
    masked = jnp.where(edge, 0.0, cross)
    for j in range(ROWS):
        for k in range(COMP):
            wf[k, j] = jnp.where(edge, 0.0, spaced(far, k, row(j)))
    for r in range(1, 4):

        def write_source(k, at, value, r=r):
            far_source[k, r - 1, at] = value

        def write_scale(at, value, r=r):
            far_scale[r - 1, at] = value

        bulk_row(lambda k, at, r=r: wf[k, r, at], write_source, write_scale, count, masked)

    def w_at(k, r):
        return wf[k, r] if r < 4 else (outer if r < 6 else inner)[k, r % 2]

    def source_at(k, r):
        return far_source[k, r - 1] if r < 4 else source[k, r - 4]

    def scale_at(r):
        return far_scale[r - 1] if r < 4 else scale[r - 4]

    for r in range(1, 5):
        for k in range(COMP):
            v1_far[k, r - 1] = relaxed_row(w_at(k, r), w_at(k, r - 1), w_at(k, r + 1), source_at(k, r), scale_at(r))

    def v1_at(k, r):
        return v1_far[k, r - 1] if r < 5 else v1[k, r - 5]

    for r in range(2, 6):
        for k in range(COMP):
            w2_far[k, r - 2] = relaxed_row(v1_at(k, r), v1_at(k, r - 1), v1_at(k, r + 1), source_at(k, r), scale_at(r))
    for r in range(3, 6):

        def write_source(k, at, value, r=r):
            source2_far[k, r - 3, at] = value

        def write_scale(at, value, r=r):
            scale2_far[r - 3, at] = value

        bulk_row(
            lambda k, at, r=r: w2_far[k, r - 2, at], write_source, write_scale, count, masked if r < 4 else cross
        )

    def w2_at(k, r):
        return w2_far[k, r - 2] if r < 6 else w2[k, r - 6]

    def source2_at(k, r):
        return source2_far[k, r - 3] if r < 6 else source2[k, r - 6]

    def scale2_at(r):
        return scale2_far[r - 3] if r < 6 else scale2[r - 6]

    for r in range(3, 7):
        for k in range(COMP):
            v2_far[k, r - 3] = relaxed_row(
                w2_at(k, r), w2_at(k, r - 1), w2_at(k, r + 1), source2_at(k, r), scale2_at(r)
            )

    def v2_at(k, r):
        return v2_far[k, r - 3] if r < 7 else v2[k, r - 7]

    for r in range(4, 8):
        for k in range(COMP):
            value = relaxed_row(v2_at(k, r), v2_at(k, r - 1), v2_at(k, r + 1), source2_at(k, r), scale2_at(r))
            emit(k, row(r - 4), value)


def store_spaced(out, k, row, value):
    count = value.shape[0]
    for v in range(count):
        out[k, row, pl.ds(v, SUB, stride=count), :] = value[v]


def far_kernel(outer, inner, far, source, scale, v1, w2, source2, scale2, v2, out, *work):
    def emit(k, row, value):
        store_spaced(out, k, row, value)

    far_rows(outer, inner, far, source, scale, v1, w2, source2, scale2, v2, work, emit)


def far_again_kernel(packed, far, source, scale, v1, w2, source2, scale2, v2, rest, weights, out, share, *work):
    nz = out.shape[3]
    total = [jnp.zeros((SUB, nz), jnp.float32) for _ in range(COMP)]

    def emit(k, row, value):
        store_spaced(out, k, row, value)
        total[k] = total[k] + jnp.sum(value, axis=0)

    far_rows(*halves(packed), far, source, scale, v1, w2, source2, scale2, v2, work, emit)
    again = packed_sums([jnp.sum(t, axis=0, keepdims=True) for t in total])
    value = weights[lax.axis_index("tm"), 0] * again + rest[...]
    for i in range(share.shape[0]):
        share[i] = value


def relay_kernel(parts, relaxed, share):
    del relaxed
    value = parts[0]
    for i in range(1, parts.shape[0]):
        value = value + parts[i]
    sub = lax.broadcasted_iota(jnp.int32, value.shape, 0)
    slabs = SUB // 2
    each = share.shape[0] // slabs
    for p in range(slabs):
        pair = jnp.where(sub % 2 == 0, value[2 * p : 2 * p + 1], value[2 * p + 1 : 2 * p + 2])
        for i in range(0, each, SUB):
            share[pl.ds(p * each + i, SUB), :] = pair


def residual_kernel(relaxed, again, residual, written):
    written[...] = jnp.zeros_like(written)
    slab = lax.axis_index("tm")
    for k in range(COMP):
        mine = relaxed[k]
        residual[0, k] = jnp.where(slab == 0, mine, again[k]) - mine


def correct_kernel(parts, relaxed, written, corrected):
    del written
    value = parts[pl.ds(0, SUB), :]
    for i in range(SUB, parts.shape[0], SUB):
        value = value + parts[pl.ds(i, SUB), :]
    value = value + pltpu.roll(value, 4, 0)
    value = value + pltpu.roll(value, 2, 0)
    nz = value.shape[1]
    lane = lax.broadcasted_iota(jnp.int32, value.shape, 1)
    for k in range(COMP):
        spread = jnp.take_along_axis(value, (k % BLK) * (nz // BLK) + lane // BLK, axis=1)
        which = k // BLK
        corrected[0, k] = relaxed[k] + spread[which : which + 1][None]


def slot_weights(slabs, nz, cells):
    decay = 1.0 / (1.0 + STEPS_SLAB * time_step * linear_rate)
    table = np.zeros((slabs, 3, SUB, nz))
    for own in range(slabs):
        chain = (own + 1) % slabs
        slots = {2: (own, -1.0)}
        if chain + 1 < slabs:
            slots[0] = (chain + 1, 1.0)
        if chain == 0:
            slots[1] = (0, 1.0)
        for which, (slot, sign) in slots.items():
            for target in range(slot, slabs):
                table[own, which, 2 * target : 2 * target + 2] = sign * decay ** (target - slot) / cells
    return jnp.asarray(table, jnp.float32)


def f32(*shape):
    return jax.ShapeDtypeStruct(shape, jnp.float32)


def call(kernel, name, out, inputs, scratch=(), cost=None):
    vmem = pl.BlockSpec(memory_space=pltpu.VMEM)
    return pl.pallas_call(
        kernel,
        out_shape=out,
        in_specs=[vmem] * len(inputs),
        out_specs=jax.tree.map(lambda _: vmem, out),
        scratch_shapes=list(scratch),
        compiler_params=LIMIT,
        name=name,
        cost_estimate=cost,
    )(*inputs)


def per_device(q_start, guess):
    own = guess[0]
    slabs = lax.axis_size("tm")
    count = lax.axis_size("outer") * lax.axis_size("inner")
    _, rows, ny, nz = own.shape
    row = (ny // SUB, SUB, nz)
    near_pairs = [(i, i ^ 1) for i in range(count)]
    far_pairs = []
    for i in range(1, count - 1, 2):
        far_pairs += [(i, i + 1), (i + 1, i)]

    farther_pairs = [(i - 2, i) for i in range(2, count, 2)] + [(i + 2, i) for i in range(1, count - 2, 2)]

    def several(*lead):
        return f32(*lead, *row)

    def scratch(*lead):
        return pltpu.VMEM((*lead, *row), jnp.float32)

    prepared = (several(COMP, 2), several(COMP, 2), several(COMP, ROWS), several(ROWS))
    state = (several(COMP, 2), several(COMP, 2), several(COMP, 2), several(2), several(COMP, 2))
    near_scratch = (scratch(COMP, 3), scratch(3), scratch(COMP, 4), scratch(COMP, 2))
    far_scratch = (
        scratch(COMP, ROWS),
        scratch(COMP, 3),
        scratch(3),
        scratch(COMP, 4),
        scratch(COMP, 4),
        scratch(COMP, 3),
        scratch(3),
        scratch(COMP, 4),
    )

    start = jnp.where(lax.axis_index("tm") == slabs - 1, q_start, own)
    far = lax.ppermute(start, SPACE, far_pairs)
    outer, inner, source, scale = call(prepare_kernel, "prepare", prepared, (start,))
    near = [lax.ppermute(half, SPACE, near_pairs) for half in (outer, inner)]
    held, near = lax.optimization_barrier((start, near))
    kept = call(near_kernel, "near", state, (outer, inner, *near, source, scale), near_scratch, SHORT)
    farther = lax.ppermute(held, SPACE, farther_pairs)
    relaxed = call(
        far_kernel, "far", f32(*own.shape), (outer, inner, far, source, scale, *kept), far_scratch, SHORT
    )

    beyond = call(prepare_kernel, "prepare_far", prepared, (far,), (), SHORT)
    kept = call(
        beyond_kernel, "beyond", state, (*beyond[:2], outer, inner, *beyond[2:]), near_scratch, SHORT
    )
    far = call(
        far_kernel,
        "far_relaxed",
        f32(*own.shape),
        (*beyond[:2], farther, *beyond[2:], *kept),
        far_scratch,
        SHORT,
    )
    my_relaxed = lax.ppermute(relaxed, "tm", [(i, (i + 1) % slabs) for i in range(slabs)])
    weights = slot_weights(slabs, nz, count * rows * ny * BLK)
    packed, source, scale, rest = call(
        prepare_again_kernel,
        "prepare_again",
        (several(COMP, ROWS), *prepared[2:], f32(SUB, nz)),
        (relaxed, guess, weights),
        (),
        SHORT,
    )
    near = lax.ppermute(packed, SPACE, near_pairs)
    kept = call(
        near_again_kernel, "near_again", state, (packed, near, source, scale), near_scratch, SHORT
    )
    again, share = call(
        far_again_kernel,
        "far_again",
        (f32(*own.shape), f32(GROUP, SUB, nz)),
        (packed, far, source, scale, *kept, rest, weights),
        far_scratch,
    )

    my_again = lax.ppermute(again, "tm", [(i, (i + 2) % slabs) for i in range(slabs)])
    parts = lax.all_to_all(share, "inner", 0, 0)
    wide = slabs * lax.axis_size("outer")
    share = call(relay_kernel, "relay", f32(2 * wide, nz), (parts, my_relaxed), (), LONG)
    parts = lax.all_to_all(share.reshape(wide, 2, nz), ("tm", "outer"), 0, 0).reshape(2 * wide, nz)
    residual, written = call(
        residual_kernel, "residual", (f32(1, *own.shape), f32(SUB, nz)), (my_relaxed, my_again)
    )
    corrected = call(correct_kernel, "correct", f32(1, *own.shape), (parts, my_relaxed, written))
    return corrected, residual


def solution(mesh):
    slabs, count = mesh.shape["tm"], mesh.shape["space"]
    fine = Mesh(mesh.devices.reshape(slabs, count // GROUP, GROUP), ("tm", *SPACE))
    q_spec = P(None, SPACE, None, None)
    field_spec = P("tm", None, SPACE, None, None)
    return jax.shard_map(
        per_device,
        mesh=fine,
        in_specs=(q_spec, field_spec),
        out_specs=(field_spec, field_spec),
        check_vma=False,
    )
```
